128 devices in a mesh: col: 32 (over x, y, core), row: 4 (over z).
Axes of the slice: x: 4, y: 4, z: 4, core: 2. Of those that a mesh axis runs over, the one named last changes fastest.
Arguments:
- targets: float32 [4, 32, 1024, 128], P(None, 'col', 'row'), as said below
- src_panels: bfloat16 [2048, 1024, 128], P('col', 'row')
- live_counts: int32 [32], P('col'), may hold values from 1 to 64, 1024 in all
- dest_owner: int32 [2048, 4], P('col'), may hold values from 0 to 31
- relative_map: int32 [2048, 4, 8], P('col', None, 'row'), may hold values from 0 to 1, as said below
- diag_row: int32 [4, 32], replicated, may hold values from 0 to 3
- parent: int32 [3, 32], replicated, may hold values from 0 to 31
- chain_map: int32 [3, 32, 8], P(None, None, 'row'), may hold values from 0 to 1, as said below
Outputs:
- factors: float32 [4, 32, 1024, 128], P(None, 'col', 'row')
The draws below stay inside these ranges and needn't reach their ends.
Inputs may be any that keep to these rules, and one draw needn't show every extreme that they name: For each i, s and row group r, the 2 entries relative_map[i, s, r * 2 : (r + 1) * 2] are a permutation of 0 to 1; on r = diag_row[s, dest_owner[i, s]] it maps 0 to 0. For each s, k and row group r, the 2 entries chain_map[s, k, r * 2 : (r + 1) * 2] are a permutation of 0 to 1; on r = diag_row[s + 1, parent[s, k]] it maps 1 to 0. `live_counts`: the counts sum to 1024 and the largest is 64. `targets`: every diagonal block after all updates is symmetric positive definite.
All inputs are finite; a program needn't handle non-finite values. No bound on the sum of `live_counts` on one device may be relied on, other than what follows from the above.
Results may differ from the reference program's by a relative error of at most 0.0003.
Values may be sent and summed in bfloat16 or wider, within the bound.
A program may use at most 128 MiB of HBM per device.

```python
import math
import jax
import jax.numpy as jnp
import numpy as np
from jax import lax

B = 128
PB = 2
SRC = 64
STEPS = 4
N_COL = 32
N_ROW = 4


def permuted(key, leading, anchor, fixed):
    scores = jax.random.randint(key, leading + (PB,), 0, 1 << 20) * PB + jnp.arange(PB)
    ordered = jnp.argsort(scores, axis=-1, stable=True).astype(jnp.int32)
    partner = ordered[..., fixed:fixed + 1]
    swapped = jnp.where(ordered == 0, partner, ordered)
    swapped = jnp.where(jnp.arange(PB) == fixed, 0, swapped)
    groups = jnp.arange(N_ROW)[:, None]
    chosen = jnp.where(groups == anchor[..., None, None], swapped, ordered)
    return chosen.reshape(leading[:-1] + (N_ROW * PB,)).astype(jnp.int32)


def structure(key):
    folded = jax.random.fold_in(key, 4242)
    streams = jax.random.split(folded, 5)
    diag_row = jax.random.randint(streams[0], (STEPS, N_COL), 0, N_ROW).astype(jnp.int32)
    parent = jax.random.randint(streams[1], (STEPS - 1, N_COL), 0, N_COL).astype(jnp.int32)
    dest_owner = jax.random.randint(streams[2], (N_COL * SRC, STEPS), 0, N_COL).astype(jnp.int32)
    source_root = diag_row[jnp.arange(STEPS)[None, :], dest_owner]
    relative_map = permuted(streams[3], (N_COL * SRC, STEPS, N_ROW), source_root, 0)
    parent_root = diag_row[1:][jnp.arange(STEPS - 1)[:, None], parent]
    chain_map = permuted(streams[4], (STEPS - 1, N_COL, N_ROW), parent_root, 1)
    return (diag_row, parent, dest_owner, relative_map, chain_map)


def draw_diag_row(key, part):
    return structure(key)[0]


def draw_parent(key, part):
    return structure(key)[1]


def draw_dest_owner(key, part):
    return structure(key)[2]


def draw_relative_map(key, part):
    return structure(key)[3]


def draw_chain_map(key, part):
    return structure(key)[4]


def draw_src_panels(key, part):
    sigma = (SRC * B * 0.5) ** (-0.25)
    inner = jax.random.fold_in(key, 55)
    shape = (N_COL * SRC, N_ROW * PB * B, B)
    values = jax.random.truncated_normal(inner, -6.0, 6.0, shape, jnp.float32)
    return (values * sigma).astype(jnp.bfloat16)


def draw_targets(key, part):
    diag_row = structure(key)[0]
    streams = jax.random.split(jax.random.fold_in(key, 77), 3)
    level_base = math.sqrt(SRC * B * 0.5)
    off_scale = min(8.0, 0.75 * level_base / math.sqrt(B))
    shape = (STEPS, N_COL, N_ROW * PB, B, B)
    blocks = off_scale * jax.random.truncated_normal(streams[0], -6.0, 6.0, shape, jnp.float32)
    noise = jax.random.normal(streams[1], (STEPS, N_COL, B, B), jnp.float32)
    noise = (noise + jnp.swapaxes(noise, -1, -2)) * (0.15 * 6.5 * level_base / math.sqrt(2.0 * B))
    level = jax.random.uniform(streams[2], (STEPS, N_COL, 1, 1), jnp.float32, 6.0, 7.0) * level_base
    diagonal = noise + level * jnp.eye(B, dtype=jnp.float32)
    marked = jnp.arange(N_ROW * PB)[None, None, :] == (diag_row * PB)[:, :, None]
    combined = jnp.where(marked[..., None, None], diagonal[:, :, None], blocks)
    return combined.reshape(STEPS, N_COL, N_ROW * PB * B, B)


def length_profile(number_of, total, reach, skew):
    loads = [(1 << 20) // math.isqrt(rank ** skew) + 1 for rank in range(2, number_of + 1)]
    rest, holding = total - reach - (number_of - 1), [1] * (number_of - 1)
    while rest > 0:
        movable = [i for i in range(number_of - 1) if holding[i] < reach]
        pool, budget = sum([loads[i] for i in movable]), rest
        for i in movable:
            addition = min(reach - holding[i], max(1, budget * loads[i] // pool), rest)
            holding[i] = holding[i] + addition
            rest = rest - addition
    return np.array([reach] + holding)


def uneven(own_key, count, total, most, lean):
    if count == 2:
        one = jax.random.randint(own_key, (), max(1, total - most), min(most, total - 1) + 1)
        return jnp.stack([one, total - one])
    lengths = jnp.asarray(length_profile(count, total, most, lean), jnp.int32)
    pairs = (count - 1) // 2
    giver, taker = lengths[1:1 + 2 * pairs:2], lengths[2:2 + 2 * pairs:2]
    slack = jnp.minimum(giver - 1, most - taker)
    passed = jax.random.randint(jax.random.fold_in(own_key, 1), (pairs,), 0, 1 << 20) % (slack + 1)
    lengths = lengths.at[1:1 + 2 * pairs:2].set(giver - passed).at[2:2 + 2 * pairs:2].set(taker + passed)
    return lengths[jax.random.permutation(jax.random.fold_in(own_key, 2), count)]


def setup_inputs(seed: int = 0) -> dict:
    seeds = jax.random.split(jax.random.key(seed), 9)
    return {
        "targets": draw_targets(jax.random.fold_in(seeds[8], 71), 0),
        "src_panels": draw_src_panels(jax.random.fold_in(seeds[8], 71), 0),
        "live_counts": uneven(seeds[2], N_COL, N_COL * SRC // 2, SRC, 2).astype(jnp.int32),
        "dest_owner": draw_dest_owner(jax.random.fold_in(seeds[8], 71), 0),
        "relative_map": draw_relative_map(jax.random.fold_in(seeds[8], 71), 0),
        "diag_row": draw_diag_row(jax.random.fold_in(seeds[8], 71), 0),
        "parent": draw_parent(jax.random.fold_in(seeds[8], 71), 0),
        "chain_map": draw_chain_map(jax.random.fold_in(seeds[8], 71), 0),
    }


def lower_solve(lower_block, blocks):
    return lax.linalg.triangular_solve(jnp.broadcast_to(lower_block[:, None], blocks.shape), blocks, left_side=False, lower=True, transpose_a=True)

def reference(targets, src_panels, live_counts, dest_owner, relative_map, diag_row, parent, chain_map):
    total_blocks = N_ROW * PB
    owners = jnp.arange(N_COL)
    panels = src_panels.reshape(N_COL, SRC, total_blocks, B, B)
    alive_mask = (jnp.arange(SRC)[None, :] < live_counts[:, None]).astype(jnp.float32)
    group_of = (jnp.arange(total_blocks) // PB).astype(jnp.int32)
    source_root = diag_row[jnp.arange(STEPS)[None, :], dest_owner].reshape(N_COL, SRC, STEPS)
    dest_grid = dest_owner.reshape(N_COL, SRC, STEPS)
    map_grid = relative_map.reshape(N_COL, SRC, STEPS, total_blocks)
    results = []
    for s in range(STEPS):

        def add_owner(running, inputs):
            panel_set, root_rows, targets_of, local_map, alive_row = inputs
            columns = panel_set[jnp.arange(SRC), root_rows * PB]
            products = jnp.einsum('ijab,icb->ijac', panel_set.astype(jnp.float32), columns.astype(jnp.float32))
            products = products * alive_row[:, None, None, None]
            slot_ids = targets_of[:, None] * total_blocks + group_of[None, :] * PB + local_map
            summed = jax.ops.segment_sum(products.reshape(SRC * total_blocks, B, B), slot_ids.reshape(-1), num_segments=N_COL * total_blocks)
            return (running + summed, None)
        update = lax.scan(add_owner, jnp.zeros((N_COL * total_blocks, B, B), jnp.float32), (panels, source_root[:, :, s], dest_grid[:, :, s], map_grid[:, :, s], alive_mask))[0]
        if s > 0:
            child_rows = results[-1].astype(jnp.bfloat16).reshape(N_COL, total_blocks, B, B)
            parent_root = diag_row[s, parent[s - 1]]
            column = child_rows[owners, parent_root * PB + 1]
            products = jnp.einsum('kjab,kcb->kjac', child_rows.astype(jnp.float32), column.astype(jnp.float32))
            kept_mask = jnp.arange(total_blocks)[None, :] != (diag_row[s - 1] * PB)[:, None]
            products = products * kept_mask[:, :, None, None].astype(jnp.float32)
            slot_ids = parent[s - 1][:, None] * total_blocks + group_of[None, :] * PB + chain_map[s - 1]
            update = update + jax.ops.segment_sum(products.reshape(N_COL * total_blocks, B, B), slot_ids.reshape(-1), num_segments=N_COL * total_blocks)
        updated = targets[s].reshape(N_COL, total_blocks, B, B) - update.reshape(N_COL, total_blocks, B, B)
        root_block = diag_row[s] * PB
        lower_block = jnp.linalg.cholesky(updated[owners, root_block])
        solved = lower_solve(lower_block, updated)
        is_diag = (jnp.arange(total_blocks)[None, :] == root_block[:, None])[:, :, None, None]
        factor = jnp.where(is_diag, lower_block[:, None], solved)
        results.append(factor.reshape(N_COL, total_blocks * B, B))
    return jnp.stack(results)
```

```python
import functools

import jax
import jax.numpy as jnp
from jax import lax
from jax.experimental import pallas as pl
from jax.experimental.pallas import tpu as pltpu
from jax.sharding import PartitionSpec as P

F32 = jnp.float32
BF16 = jnp.bfloat16
B = 128
TRANS_B = (((1,), (1,)), ((), ()))
TRANS_A = (((0,), (0,)), ((), ()))
VMEM = pl.BlockSpec(memory_space=pltpu.VMEM)
SMEM = pl.BlockSpec(memory_space=pltpu.SMEM)


def cholesky_inverse(a):
    n = a.shape[0]
    lane = lax.broadcasted_iota(jnp.int32, (8, n), 1)
    sub = lax.broadcasted_iota(jnp.int32, (8, n), 0)
    upper, inverse = [], []
    w = None
    for j in range(n // 8):
        pa = a[:8]
        pw = (lane == sub + 8 * j).astype(F32)
        if w is not None:
            pw = pw + w[:8]
        pivots = jnp.zeros((8, n), F32)
        for t in range(8):
            col = jnp.broadcast_to(pa[:, 8 * j + t : 8 * j + t + 1], (8, n))
            d = jnp.broadcast_to(col[t : t + 1], (8, n))
            pivots = jnp.where(sub == t, d, pivots)
            if t < 7:
                factor = jnp.where(sub > t, col / d, 0.0)
                pa = pa - factor * pa[t : t + 1]
                pw = pw - factor * pw[t : t + 1]
        scale = lax.rsqrt(pivots)
        scale = scale * (1.5 - 0.5 * pivots * scale * scale)
        pa = jnp.where(lane >= sub + 8 * j, pa * scale, 0.0)
        pw = pw * scale
        upper.append(pa)
        inverse.append(pw)
        if j + 1 < n // 8:
            both = jnp.concatenate([pa, pw], axis=1)
            step = lax.dot_general(
                pa[:, 8 * j + 8 :] if (8 * j + 8) % 128 == 0 else pa, both, TRANS_A,
                precision=lax.Precision.HIGHEST, preferred_element_type=F32,
            )[8 * j + 8 :]
            a = a[8:] - step[:, :n]
            w = -step[:, n:] if w is None else w[8:] - step[:, n:]
    return jnp.concatenate(upper, axis=0).T, jnp.concatenate(inverse, axis=0)


def products_kernel(steps, live_ref, dest_ref, map_ref, root_ref, panel_ref, head_ref, out_ref):
    s = pl.program_id(0)
    out_ref[...] = jnp.zeros_like(out_ref)

    @pl.loop(0, live_ref[0])
    def _(i):
        dest = dest_ref[i, s]
        first = map_ref[i, s, 0]
        prod = lax.dot_general(panel_ref[i], head_ref[root_ref[i, s], i], TRANS_B, preferred_element_type=F32)
        top = pl.multiple_of(first * B, B)
        low = pl.multiple_of(B - first * B, B)
        out_ref[0, dest, pl.ds(top, B), :] += prod[:B]
        out_ref[0, dest, pl.ds(low, B), :] += prod[B:]


def slot_sums(live, dest, maps, roots, panels, heads, col_count):
    src, rows, width = panels.shape
    steps = dest.shape[1]
    return pl.pallas_call(
        functools.partial(products_kernel, steps),
        grid=(steps,),
        out_shape=jax.ShapeDtypeStruct((steps, col_count, rows, width), F32),
        in_specs=[SMEM, SMEM, SMEM, SMEM, VMEM, VMEM],
        out_specs=pl.BlockSpec((1, col_count, rows, width), lambda s: (s, 0, 0, 0)),
        name="slot_sums",
    )(live, dest, maps, roots, panels, heads)


def factor_kernel(first_step, place_ref, parent_ref, map_ref, before_ref, base_ref, diag_ref, child_ref, out_ref, low_ref, upd, dg):
    owner, is_root, row = place_ref[0], place_ref[1], place_ref[2]
    upd[...] = base_ref[...]
    dg[...] = diag_ref[...]
    if not first_step:

        @pl.loop(0, parent_ref.shape[0])
        def _(k):
            @pl.when(parent_ref[k] == owner)
            def _():
                head = child_ref[k, 2 * B :]
                prod = lax.dot_general(child_ref[k, : 2 * B], head, TRANS_B, preferred_element_type=F32)
                dg[...] -= lax.dot_general(head, head, TRANS_B, preferred_element_type=F32)
                first = map_ref[k, 0]
                top = pl.multiple_of(first * B, B)
                low = pl.multiple_of(B - first * B, B)
                upd[pl.ds(low, B), :] -= prod[B:]

                @pl.when(before_ref[k] != row)
                def _():
                    upd[pl.ds(top, B), :] -= prod[:B]

    lower, inverse = cholesky_inverse(dg[...])
    solved = lax.dot_general(
        upd[...], inverse, TRANS_B, precision=lax.Precision.HIGHEST, preferred_element_type=F32
    )
    out_ref[...] = solved

    @pl.when(is_root == 1)
    def _():
        out_ref[:B] = lower

    low_ref[...] = out_ref[...].astype(BF16)


def factor(first_step, place, parent, maps, before, base, diag, child):
    rows, width = base.shape
    return pl.pallas_call(
        functools.partial(factor_kernel, first_step),
        out_shape=[jax.ShapeDtypeStruct((rows, width), F32), jax.ShapeDtypeStruct((rows, width), BF16)],
        in_specs=[SMEM, SMEM, SMEM, SMEM, VMEM, VMEM, VMEM],
        out_specs=[VMEM, VMEM],
        scratch_shapes=[pltpu.VMEM((rows, width), F32), pltpu.VMEM((B, width), F32)],
        name="factor_first" if first_step else "factor_next",
    )(place, parent, maps, before, base, diag, child)


def local(targets, src_panels, live_counts, dest_owner, relative_map, diag_row, parent, chain_map):
    cols = lax.axis_size("col")
    owner = lax.axis_index("col")
    row = lax.axis_index("row")
    src, rows, width = src_panels.shape
    steps = targets.shape[0]
    heads = lax.all_gather(src_panels[:, :B], "row", axis=0)
    roots = diag_row[jnp.arange(steps)[None, :], dest_owner]
    sums = slot_sums(live_counts, dest_owner, relative_map, roots, src_panels, heads, cols)
    bases, diags = [], []
    for s in range(steps):
        got = lax.psum_scatter(sums[s], "col", scatter_dimension=0, tiled=False)
        base = targets[s, 0] - got
        bases.append(base)
        diags.append(lax.all_gather(base[:B], "row", axis=0)[diag_row[s, owner]])
    results = []
    child = jnp.zeros((1, 8, width), BF16)
    for s in range(steps):
        t = max(s - 1, 0)
        place = jnp.stack([owner, (diag_row[s, owner] == row).astype(jnp.int32), row])
        out, low = factor(s == 0, place, parent[t], chain_map[t], diag_row[t], bases[s], diags[s], child)
        results.append(out)
        if s + 1 < steps:
            gathered = lax.all_gather(low[B:], "row", axis=0)
            head = gathered[diag_row[s + 1, parent[s, owner]]]
            child = lax.all_gather(jnp.concatenate([low, head], axis=0), "col", axis=0)
    return jnp.stack(results)[:, None]


def solution(mesh):
    return jax.shard_map(
        local,
        mesh=mesh,
        in_specs=(
            P(None, "col", "row", None),
            P("col", "row", None),
            P("col"),
            P("col", None),
            P("col", None, "row"),
            P(),
            P(),
            P(None, None, "row"),
        ),
        out_specs=P(None, "col", "row", None),
        check_vma=False,
    )
```

```python
import functools

import jax
import jax.numpy as jnp
from jax import lax
from jax.experimental import pallas as pl
from jax.experimental.pallas import tpu as pltpu
from jax.sharding import PartitionSpec as P

F32 = jnp.float32
BF16 = jnp.bfloat16
B = 128
TRANS_B = (((1,), (1,)), ((), ()))
TRANS_A = (((0,), (0,)), ((), ()))
VMEM = pl.BlockSpec(memory_space=pltpu.VMEM)
MESH = pl.DeviceIdType.MESH
SMEM = pl.BlockSpec(memory_space=pltpu.SMEM)


def cholesky_inverse(a):
    n = a.shape[0]
    lane = lax.broadcasted_iota(jnp.int32, (8, n), 1)
    sub = lax.broadcasted_iota(jnp.int32, (8, n), 0)
    upper, inverse = [], []
    w = None
    for j in range(n // 8):
        pa = a[:8]
        pw = (lane == sub + 8 * j).astype(F32)
        if w is not None:
            pw = pw + w[:8]
        pivots = jnp.zeros((8, n), F32)
        for t in range(8):
            col = jnp.broadcast_to(pa[:, 8 * j + t : 8 * j + t + 1], (8, n))
            d = jnp.broadcast_to(col[t : t + 1], (8, n))
            pivots = jnp.where(sub == t, d, pivots)
            if t < 7:
                factor = jnp.where(sub > t, col / d, 0.0)
                pa = pa - factor * pa[t : t + 1]
                pw = pw - factor * pw[t : t + 1]
        scale = lax.rsqrt(pivots)
        scale = scale * (1.5 - 0.5 * pivots * scale * scale)
        pa = jnp.where(lane >= sub + 8 * j, pa * scale, 0.0)
        pw = pw * scale
        upper.append(pa)
        inverse.append(pw)
        if j + 1 < n // 8:
            both = jnp.concatenate([pa, pw], axis=1)
            step = lax.dot_general(
                pa[:, 8 * j + 8 :] if (8 * j + 8) % 128 == 0 else pa, both, TRANS_A,
                precision=lax.Precision.HIGHEST, preferred_element_type=F32,
            )[8 * j + 8 :]
            a = a[8:] - step[:, :n]
            w = -step[:, n:] if w is None else w[8:] - step[:, n:]
    return jnp.concatenate(upper, axis=0).T, jnp.concatenate(inverse, axis=0)


def products_kernel(steps, live_ref, dest_ref, map_ref, root_ref, panel_ref, head_ref, out_ref):
    s = pl.program_id(0)
    out_ref[...] = jnp.zeros_like(out_ref)

    @pl.loop(0, live_ref[0])
    def _(i):
        dest = dest_ref[i, s]
        first = map_ref[i, s, 0]
        prod = lax.dot_general(panel_ref[i], head_ref[root_ref[i, s], i], TRANS_B, preferred_element_type=F32)
        top = pl.multiple_of(first * B, B)
        low = pl.multiple_of(B - first * B, B)
        out_ref[0, dest, pl.ds(top, B), :] += prod[:B]
        out_ref[0, dest, pl.ds(low, B), :] += prod[B:]


def slot_sums(live, dest, maps, roots, panels, heads, col_count):
    src, rows, width = panels.shape
    steps = dest.shape[1]
    return pl.pallas_call(
        functools.partial(products_kernel, steps),
        grid=(steps,),
        out_shape=jax.ShapeDtypeStruct((steps, col_count, rows, width), F32),
        in_specs=[SMEM, SMEM, SMEM, SMEM, VMEM, VMEM],
        out_specs=pl.BlockSpec((1, col_count, rows, width), lambda s: (s, 0, 0, 0)),
        name="slot_sums",
    )(live, dest, maps, roots, panels, heads)


def factor_kernel(first_step, place_ref, parent_ref, map_ref, before_ref, base_ref, diag_ref, child_ref, out_ref, low_ref, upd, dg):
    owner, is_root, row = place_ref[0], place_ref[1], place_ref[2]
    upd[...] = base_ref[...]
    dg[...] = diag_ref[...]
    if not first_step:

        @pl.loop(0, parent_ref.shape[0])
        def _(k):
            @pl.when(parent_ref[k] == owner)
            def _():
                parts = [child_ref[h, k, b] for b in range(3) for h in range(2)]
                head = jnp.concatenate(parts[4:], axis=0)
                prod = lax.dot_general(jnp.concatenate(parts[:4], axis=0), head, TRANS_B, preferred_element_type=F32)
                dg[...] -= lax.dot_general(head, head, TRANS_B, preferred_element_type=F32)
                first = map_ref[k, 0]
                top = pl.multiple_of(first * B, B)
                low = pl.multiple_of(B - first * B, B)
                upd[pl.ds(low, B), :] -= prod[B:]

                @pl.when(before_ref[k] != row)
                def _():
                    upd[pl.ds(top, B), :] -= prod[:B]

    lower, inverse = cholesky_inverse(dg[...])
    solved = lax.dot_general(
        upd[...], inverse, TRANS_B, precision=lax.Precision.HIGHEST, preferred_element_type=F32
    )
    out_ref[...] = solved

    @pl.when(is_root == 1)
    def _():
        out_ref[:B] = lower

    low_ref[...] = out_ref[...].astype(BF16)


def factor(step, place, parent, maps, before, base, diag, child):
    rows, width = base.shape[1:]
    return pl.pallas_call(
        functools.partial(factor_kernel, step == 0),
        grid=(1,),
        out_shape=[jax.ShapeDtypeStruct((rows, width), F32), jax.ShapeDtypeStruct((rows, width), BF16)],
        in_specs=[
            SMEM, SMEM, SMEM, SMEM,
            pl.BlockSpec((None, rows, width), lambda i: (step, 0, 0)),
            pl.BlockSpec((None, B, width), lambda i: (step, 0, 0)),
            VMEM,
        ],
        out_specs=[VMEM, VMEM],
        scratch_shapes=[pltpu.VMEM((rows, width), F32), pltpu.VMEM((B, width), F32)],
        name="factor_first" if step == 0 else "factor_next",
    )(place, parent, maps, before, base, diag, child)


def position():
    me = lax.axis_index("col")
    return me // 8, lax.rem(me // 2, 4), lax.rem(me, 2), lax.axis_index("row")


def at_x(d):
    x, y, p, _ = position()
    return lax.rem(x + d, 4), {"col": (lax.rem(x + d, 4) * 4 + y) * 2 + p}


def at_y(d):
    x, y, p, _ = position()
    return lax.rem(y + d, 4), {"col": (x * 4 + lax.rem(y + d, 4)) * 2 + p}


def at_z(d):
    return {"row": lax.rem(lax.axis_index("row") + d, 4)}


def partner():
    x, y, p, _ = position()
    return {"col": (x * 4 + y) * 2 + 1 - p}


def greet():
    barrier = pltpu.get_barrier_semaphore()
    peers = [partner()] + [at_z(d) for d in (1, 2, 3)] + [f(d)[1] for f in (at_x, at_y) for d in (1, 2, 3)]
    for peer in peers:
        pl.semaphore_signal(barrier, inc=1, device_id=peer, device_id_type=MESH)
    pl.semaphore_wait(barrier, len(peers))


class Copies:
    def __init__(self, send, recv):
        self.send, self.recv, self.all = send, recv, []

    def start(self, src, dst, peer):
        n = len(self.all)
        copy = pltpu.make_async_remote_copy(
            src_ref=src, dst_ref=dst, send_sem=self.send.at[n], recv_sem=self.recv.at[n], device_id=peer, device_id_type=MESH
        )
        copy.start()
        self.all.append(copy)
        return copy

    def finish(self):
        for copy in self.all:
            copy.wait_send()


def scatter_kernel(root_ref, sums, target_ref, base_ref, diag_ref, acc, in0, part, in1, in2, zbuf, load_sem, send_sem, recv_sem):
    steps = sums.shape[0]
    x, y, p, row = position()
    copies = Copies(send_sem, recv_sem)
    loads, first, second, third, fourth = {}, {}, {}, {}, {}
    for s in range(steps):
        loads[s] = pltpu.make_async_copy(sums.at[s, :, :, p], acc.at[s], load_sem.at[s])
        loads[s].start()
    greet()
    for s in range(steps):
        first[s] = copies.start(sums.at[s, :, :, 1 - p], in0.at[s], partner())

    def pair(s):
        loads[s].wait()
        first[s].wait_recv()

        @pl.loop(0, 16)
        def _(i):
            acc[s, i // 4, lax.rem(i, 4)] += in0[s, i // 4, lax.rem(i, 4)]

        second[s] = []
        for d in (2, 1, 3):
            to, peer = at_x(d)
            second[s].append(copies.start(acc.at[s, to, :, :B], in1.at[s, 0, d - 1], peer))
            to, peer = at_y(d)
            second[s].append(copies.start(acc.at[s, :, to, B:], in1.at[s, 1, d - 1], peer))

    def cross(s):
        for copy in second[s]:
            copy.wait_recv()

        @pl.loop(0, 4)
        def _(i):
            part[s, 0, i] = acc[s, x, i, :B] + in1[s, 0, 0, i] + in1[s, 0, 1, i] + in1[s, 0, 2, i]
            part[s, 1, i] = acc[s, i, y, B:] + in1[s, 1, 0, i] + in1[s, 1, 1, i] + in1[s, 1, 2, i]

        third[s] = []
        for d in (2, 1, 3):
            to, peer = at_y(d)
            third[s].append(copies.start(part.at[s, 0, to], in2.at[s, 0, d - 1], peer))
            to, peer = at_x(d)
            third[s].append(copies.start(part.at[s, 1, to], in2.at[s, 1, d - 1], peer))

    def finish(s):
        for copy in third[s]:
            copy.wait_recv()
        base = target_ref[s, :B] - (part[s, 0, y] + in2[s, 0, 0] + in2[s, 0, 1] + in2[s, 0, 2])
        base_ref[s, :B] = base
        zbuf[s, row] = base
        base_ref[s, B:] = target_ref[s, B:] - (part[s, 1, x] + in2[s, 1, 0] + in2[s, 1, 1] + in2[s, 1, 2])
        fourth[s] = [copies.start(zbuf.at[s, row], zbuf.at[s, row], at_z(d)) for d in (2, 1, 3)]

    for t in range(steps + 2):
        if t < steps:
            pair(t)
        if 0 <= t - 1 < steps:
            cross(t - 1)
        if 0 <= t - 2 < steps:
            finish(t - 2)
    for s in range(steps):
        for copy in fourth[s]:
            copy.wait_recv()
    for s in range(steps):
        diag_ref[s] = zbuf[s, root_ref[s]]
    copies.finish()


def scatter_reduce(roots, sums, targets):
    steps, rows, width = targets.shape
    count = steps * 16
    return pl.pallas_call(
        scatter_kernel,
        out_shape=[jax.ShapeDtypeStruct((steps, rows, width), F32), jax.ShapeDtypeStruct((steps, B, width), F32)],
        in_specs=[SMEM, pl.BlockSpec(memory_space=pl.ANY), VMEM],
        out_specs=[VMEM, VMEM],
        scratch_shapes=[
            pltpu.VMEM((steps, 4, 4, rows, width), F32),
            pltpu.VMEM((steps, 4, 4, rows, width), F32),
            pltpu.VMEM((steps, 2, 4, B, width), F32),
            pltpu.VMEM((steps, 2, 3, 4, B, width), F32),
            pltpu.VMEM((steps, 2, 3, B, width), F32),
            pltpu.VMEM((steps, 4, B, width), F32),
            pltpu.SemaphoreType.DMA((steps,)),
            pltpu.SemaphoreType.DMA((count,)),
            pltpu.SemaphoreType.DMA((count,)),
        ],
        compiler_params=pltpu.CompilerParams(collective_id=0, has_side_effects=True),
        name="scatter_reduce",
    )(roots, sums.reshape(steps, 4, 4, 2, rows, width), targets)


def exchange_kernel(root_ref, low, out, zbuf, send_sem, recv_sem):
    x, y, p, row = position()
    copies = Copies(send_sem, recv_sem)
    for h in range(2):
        out[h, x, y, p, :2] = low[:, h]
    zbuf[row] = low[1]
    greet()
    rows, head = slice(0, 2), slice(2, 3)
    heads = [copies.start(low.at[1], zbuf.at[row], at_z(d)) for d in (2, 1, 3)]

    def open_half(h, what, src):
        move = at_y if h else at_x
        return [copies.start(src, out.at[h, x, y, p, what], move(d)[1]) for d in (2, 1, 3)]

    def line(h, fixed, what):
        return out.at[1, fixed, :, p, what] if h else out.at[0, :, fixed, p, what]

    def turn(h, what, opened):
        for copy in opened:
            copy.wait_recv()
        move, here = (at_x, x) if h else (at_y, y)
        ref = line(h, here, what)
        return [copies.start(ref, ref, move(d)[1]) for d in (2, 1, 3)], copies.start(ref, ref, partner())

    def close(h, what, turned):
        done = [turned[1]]
        move = at_x if h else at_y
        for d, copy in zip((2, 1, 3), turned[0]):
            copy.wait_recv()
            ref = line(h, move(4 - d)[0], what)
            done.append(copies.start(ref, ref, partner()))
        return done

    opened = [open_half(h, rows, low.at[:, h]) for h in range(2)]
    for copy in heads:
        copy.wait_recv()
    picked = zbuf[root_ref[0]]
    for h in range(2):
        out[h, x, y, p, 2] = picked[h]
    opened_head = [open_half(h, head, out.at[h, x, y, p, head]) for h in range(2)]
    turned = [turn(h, rows, opened[h]) for h in range(2)]
    turned_head = [turn(h, head, opened_head[h]) for h in range(2)]
    done = []
    for h in range(2):
        done += close(h, rows, turned[h])
    for h in range(2):
        done += close(h, head, turned_head[h])
    for copy in done:
        copy.wait_recv()
    copies.finish()


def exchange(root, low):
    width = low.shape[1]
    out = pl.pallas_call(
        exchange_kernel,
        out_shape=jax.ShapeDtypeStruct((2, 4, 4, 2, 3, B // 2, width), BF16),
        in_specs=[SMEM, VMEM],
        out_specs=VMEM,
        scratch_shapes=[
            pltpu.VMEM((4, 2, B // 2, width), BF16),
            pltpu.SemaphoreType.DMA((43,)),
            pltpu.SemaphoreType.DMA((43,)),
        ],
        compiler_params=pltpu.CompilerParams(collective_id=1, has_side_effects=True),
        name="exchange",
    )(root, low.reshape(2, 2, B // 2, width))
    return out.reshape(2, 32, 3, B // 2, width)


def local(targets, src_panels, live_counts, dest_owner, relative_map, diag_row, parent, chain_map):
    cols = lax.axis_size("col")
    owner = lax.axis_index("col")
    row = lax.axis_index("row")
    width = src_panels.shape[2]
    steps = targets.shape[0]
    heads = lax.all_gather(src_panels[:, :B], "row", axis=0)
    roots = diag_row[jnp.arange(steps)[None, :], dest_owner]
    sums = slot_sums(live_counts, dest_owner, relative_map, roots, src_panels, heads, cols)
    base, diag = scatter_reduce(diag_row[:, owner], sums, targets[:, 0])
    results = []
    child = jnp.zeros((2, 1, 3, 8, width), BF16)
    for s in range(steps):
        t = max(s - 1, 0)
        place = jnp.stack([owner, (diag_row[s, owner] == row).astype(jnp.int32), row])
        out, low = factor(s, place, parent[t], chain_map[t], diag_row[t], base, diag, child)
        results.append(out)
        if s + 1 < steps:
            child = exchange(diag_row[s + 1, parent[s, owner]].reshape(1), low)
    return jnp.stack(results)[:, None]


def solution(mesh):
    return jax.shard_map(
        local,
        mesh=mesh,
        in_specs=(
            P(None, "col", "row", None),
            P("col", "row", None),
            P("col"),
            P("col", None),
            P("col", None, "row"),
            P(),
            P(),
            P(None, None, "row"),
        ),
        out_specs=P(None, "col", "row", None),
        check_vma=False,
    )
```

```python
import functools

import jax
import jax.numpy as jnp
from jax import lax
from jax.experimental import pallas as pl
from jax.experimental.pallas import tpu as pltpu
from jax.sharding import PartitionSpec as P

F32 = jnp.float32
BF16 = jnp.bfloat16
B = 128
H = B // 2
WIRE = F32
TRANS_B = (((1,), (1,)), ((), ()))
TRANS_A = (((0,), (0,)), ((), ()))
MESH = pl.DeviceIdType.MESH
VMEM = pl.BlockSpec(memory_space=pltpu.VMEM)
SMEM = pl.BlockSpec(memory_space=pltpu.SMEM)
ANY = pl.BlockSpec(memory_space=pl.ANY)


def split_product(left, right):
    def parts(v):
        high = v.astype(BF16).astype(F32)
        mid = (v - high).astype(BF16).astype(F32)
        return high, mid, v - high - mid

    lh, lm, ll = parts(left)
    rh, rm, rl = parts(right)
    lefts = jnp.concatenate([lh, lh, lm, lh, ll, lm], axis=0).astype(BF16)
    rights = jnp.concatenate([rh, rm, rh, rl, rh, rm], axis=0).astype(BF16)
    return lax.dot_general(lefts, rights, TRANS_A, preferred_element_type=F32)


def cholesky_inverse(a):
    n = a.shape[0]
    lane = lax.broadcasted_iota(jnp.int32, (8, n), 1)
    sub = lax.broadcasted_iota(jnp.int32, (8, n), 0)
    upper, inverse = [], []
    next_a, rest_a, next_w, rest_w = a[:8], a[8:], None, None
    for j in range(n // 8):
        pa = next_a
        pw = (lane == sub + 8 * j).astype(F32)
        if next_w is not None:
            pw = pw + next_w
        cols = [jnp.broadcast_to(pa[:, 8 * j + t : 8 * j + t + 1], (8, n)) for t in range(8)]
        pivots = jnp.zeros((8, n), F32)
        for t in range(8):
            d = jnp.broadcast_to(cols[t][t : t + 1], (8, n))
            pivots = jnp.where(sub == t, d, pivots)
            if t < 7:
                ratio = jnp.where(sub > t, cols[t] * (1.0 / d), 0.0)
                for v in range(t + 1, 8):
                    cols[v] = cols[v] - ratio * cols[v][t : t + 1]
                pa = pa - ratio * pa[t : t + 1]
                pw = pw - ratio * pw[t : t + 1]
        scale = lax.rsqrt(pivots)
        scale = scale * (1.5 - 0.5 * pivots * scale * scale)
        pa = jnp.where(lane >= sub + 8 * j, pa * scale, 0.0)
        pw = pw * scale
        upper.append(pa)
        inverse.append(pw)
        if j + 1 < n // 8:
            both = jnp.concatenate([pa, pw], axis=1)
            first = split_product(pa[:, 8 * j + 8 : 8 * j + 16], both)
            next_a = rest_a[:8] - first[:, :n]
            next_w = -first[:, n:] if rest_w is None else rest_w[:8] - first[:, n:]
            if j + 2 < n // 8:
                step = split_product(pa[:, 8 * j + 16 :], both)
                rest_a = rest_a[8:] - step[:, :n]
                rest_w = -step[:, n:] if rest_w is None else rest_w[8:] - step[:, n:]
    return jnp.concatenate(upper, axis=0).T, jnp.concatenate(inverse, axis=0)


def products_kernel(step, live_ref, dest_ref, map_ref, panel_ref, head_ref, out_ref):
    live = live_ref[0]

    @pl.loop(0, out_ref.shape[0])
    def _(c):
        out_ref[c] = jnp.zeros(out_ref.shape[1:], F32)

    @pl.loop(0, (live + 3) // 4)
    def _(g):
        prods = []
        for u in range(4):
            i = g * 4 + u
            head = head_ref[i]
            head = jnp.where(i < live, head, jnp.zeros_like(head))
            prods.append(lax.dot_general(panel_ref[i], head, TRANS_B, preferred_element_type=F32))
        for u in range(4):
            i = g * 4 + u
            dest, first = dest_ref[i, step], map_ref[i, step * 2]
            out_ref[dest, pl.ds(pl.multiple_of(first * B, B), B), :] += prods[u][:B]
            out_ref[dest, pl.ds(pl.multiple_of(B - first * B, B), B), :] += prods[u][B:]


def slot_sums(step, live, dest, maps, panels, heads, col_count):
    src, rows, width = panels.shape
    return pl.pallas_call(
        functools.partial(products_kernel, step),
        out_shape=jax.ShapeDtypeStruct((col_count, rows, width), F32),
        in_specs=[SMEM, SMEM, SMEM, VMEM, VMEM],
        out_specs=VMEM,
        name="slot_sums",
    )(live, dest, maps, panels, heads.reshape(src, B, width))


def factor_kernel(step, parent_ref, map_ref, root_ref, base_ref, diag_ref, child_ref, *rest):
    out_ref, low_ref, upd, dg = rest[-4:]
    owner, row = lax.axis_index("col"), lax.axis_index("row")
    upd[...] = base_ref[...]
    dg[...] = diag_ref[...]
    if step:

        @pl.loop(0, parent_ref.shape[1])
        def _(k):
            @pl.when(parent_ref[step - 1, k] == owner)
            def _():
                parts = [child_ref[h, k, b] for b in range(3) for h in range(2)]
                head = jnp.concatenate(parts[4:], axis=0)
                prod = lax.dot_general(jnp.concatenate(parts[:4], axis=0), head, TRANS_B, preferred_element_type=F32)
                dg[...] -= lax.dot_general(head, head, TRANS_B, preferred_element_type=F32)
                first = map_ref[step - 1, k * 2]
                top = pl.multiple_of(first * B, B)
                low = pl.multiple_of(B - first * B, B)
                upd[pl.ds(low, B), :] -= prod[B:]

                @pl.when(root_ref[step - 1, k] != row)
                def _():
                    upd[pl.ds(top, B), :] -= prod[:B]

    lower, inverse = cholesky_inverse(dg[...])
    out_ref[...] = lax.dot_general(
        upd[...], inverse, TRANS_B, precision=lax.Precision.HIGHEST, preferred_element_type=F32
    )

    @pl.when(root_ref[step, owner] == row)
    def _():
        out_ref[:B] = lower

    low_ref[...] = out_ref[...].astype(BF16)


def factor(step, steps, parent, maps, roots, base, diag, child, panels):
    rows, width = base.shape
    whole = jax.ShapeDtypeStruct((steps, rows, width), F32)
    operands = [parent, maps, roots, base, diag, child] + ([panels] if step else [])
    return pl.pallas_call(
        functools.partial(factor_kernel, step),
        grid=(1,),
        out_shape=[whole, jax.ShapeDtypeStruct((rows, width), BF16)],
        in_specs=[SMEM, SMEM, SMEM, VMEM, VMEM, VMEM] + ([ANY] if step else []),
        out_specs=[pl.BlockSpec((None, rows, width), lambda i: (step, 0, 0)), VMEM],
        scratch_shapes=[pltpu.VMEM((rows, width), F32), pltpu.VMEM((B, width), F32)],
        input_output_aliases={6: 0} if step else {},
        name=f"factor_{step}",
    )(*operands)


def position():
    me = lax.axis_index("col")
    return me // 8, lax.rem(me // 2, 4), lax.rem(me, 2), lax.axis_index("row")


def at_x(d):
    x, y, p, _ = position()
    return lax.rem(x + d, 4), {"col": (lax.rem(x + d, 4) * 4 + y) * 2 + p}


def at_y(d):
    x, y, p, _ = position()
    return lax.rem(y + d, 4), {"col": (x * 4 + lax.rem(y + d, 4)) * 2 + p}


def at_z(d):
    return {"row": lax.rem(lax.axis_index("row") + d, 4)}


def partner():
    x, y, p, _ = position()
    return {"col": (x * 4 + y) * 2 + 1 - p}


def greet(peers):
    barrier = pltpu.get_barrier_semaphore()
    for peer in peers:
        pl.semaphore_signal(barrier, inc=1, device_id=peer, device_id_type=MESH)
    pl.semaphore_wait(barrier, len(peers))


class Copies:
    def __init__(self, send, recv):
        self.send, self.recv, self.all = send, recv, []

    def start(self, src, dst, peer):
        n = len(self.all)
        copy = pltpu.make_async_remote_copy(
            src_ref=src, dst_ref=dst, send_sem=self.send.at[n], recv_sem=self.recv.at[n], device_id=peer, device_id_type=MESH
        )
        copy.start()
        self.all.append(copy)
        return copy

    def finish(self):
        for copy in self.all:
            copy.wait_send()


class Broadcast:
    def __init__(self, copies, mine, out):
        row = lax.axis_index("row")
        self.copies, self.out = copies, out
        self.low, self.high = pl.ds(0, 8), pl.ds(8, 8)
        self.up = [copies.start(mine.at[part], out.at[row, part], at_z(1)) for part in (self.low, self.high)]
        self.down = [copies.start(mine.at[part], out.at[row, part], at_z(3)) for part in (self.high, self.low)]

    def relay(self):
        row = lax.axis_index("row")
        self.up[0].wait_recv()
        ref = self.out.at[lax.rem(row + 3, 4), self.low]
        self.on = [self.copies.start(ref, ref, at_z(1))]
        self.down[0].wait_recv()
        ref = self.out.at[lax.rem(row + 1, 4), self.high]
        self.on.append(self.copies.start(ref, ref, at_z(3)))

    def finish(self):
        for copy in [self.up[1], self.down[1]] + self.on:
            copy.wait_recv()


def open_kernel(dest_ref, root_ref, panels, out, chosen, zbuf, first, load_sem, send_sem, recv_sem):
    row = lax.axis_index("row")
    copies = Copies(send_sem, recv_sem)

    def quarter(q):
        return panels.at[pl.ds(q * 16, 16), pl.ds(0, B)]

    own = pltpu.make_async_copy(quarter(row), zbuf.at[row], load_sem)
    own.start()
    greet([at_z(d) for d in (1, 2, 3)])
    opened = [copies.start(quarter(lax.rem(row + d, 4)), zbuf.at[row], at_z(d)) for d in (2, 1, 3)]
    own.wait()
    for copy in opened:
        copy.wait_recv()
    steps = chosen.shape[0] + 1

    @pl.loop(0, 16)
    def _(j):
        first[j] = zbuf[root_ref[0, dest_ref[row * 16 + j, 0]], j]

    cast = Broadcast(copies, first, out)

    @pl.loop(0, 16)
    def _(j):
        out[row, j] = first[j]
        for s in range(1, steps):
            chosen[s - 1, j] = zbuf[root_ref[s, dest_ref[row * 16 + j, s]], j]

    cast.relay()
    cast.finish()
    copies.finish()


def open_heads(dest, roots, panels, steps):
    width = panels.shape[2]
    quarter = (16, B, width)
    return pl.pallas_call(
        open_kernel,
        out_shape=[jax.ShapeDtypeStruct((4,) + quarter, BF16), jax.ShapeDtypeStruct((steps - 1,) + quarter, BF16)],
        in_specs=[SMEM, SMEM, ANY],
        out_specs=[VMEM, VMEM],
        scratch_shapes=[
            pltpu.VMEM((4,) + quarter, BF16),
            pltpu.VMEM(quarter, BF16),
            pltpu.SemaphoreType.DMA,
            pltpu.SemaphoreType.DMA((9,)),
            pltpu.SemaphoreType.DMA((9,)),
        ],
        compiler_params=pltpu.CompilerParams(collective_id=0, has_side_effects=True),
        name="open_heads",
    )(dest, roots, panels)


class Exchange:
    rows, head = slice(0, 2), slice(2, 3)

    def __init__(self, copies, low, out, zbuf):
        self.copies, self.low, self.out, self.zbuf = copies, low, out, zbuf
        x, y, p, row = position()
        for h in range(2):
            out[h, x, y, p, :2] = low[:, h]
        zbuf[row] = low[1]

    def line(self, h, fixed, what):
        p = position()[2]
        return self.out.at[1, fixed, :, p, what] if h else self.out.at[0, :, fixed, p, what]

    def open_half(self, h, what, src):
        x, y, p, _ = position()
        move = at_y if h else at_x
        return [self.copies.start(src, self.out.at[h, x, y, p, what], move(d)[1]) for d in (2, 1, 3)]

    def begin(self):
        row = lax.axis_index("row")
        self.heads = [self.copies.start(self.low.at[1], self.zbuf.at[row], at_z(d)) for d in (2, 1, 3)]
        self.opened = [self.open_half(h, self.rows, self.low.at[:, h]) for h in range(2)]

    def pick(self, root):
        x, y, p, _ = position()
        for copy in self.heads:
            copy.wait_recv()
        picked = self.zbuf[root]
        for h in range(2):
            self.out[h, x, y, p, 2] = picked[h]
        self.opened_head = [self.open_half(h, self.head, self.out.at[h, x, y, p, self.head]) for h in range(2)]

    def turn_half(self, h, what, opened):
        x, y, _, _ = position()
        for copy in opened:
            copy.wait_recv()
        move, here = (at_x, x) if h else (at_y, y)
        ref = self.line(h, here, what)
        return [self.copies.start(ref, ref, move(d)[1]) for d in (2, 1, 3)], self.copies.start(ref, ref, partner())

    def turn(self):
        self.turned = [self.turn_half(h, self.rows, self.opened[h]) for h in range(2)]
        self.turned_head = [self.turn_half(h, self.head, self.opened_head[h]) for h in range(2)]

    def close_half(self, h, what, turned):
        self.done.append(turned[1])
        move = at_x if h else at_y
        for d, copy in zip((2, 1, 3), turned[0]):
            copy.wait_recv()
            ref = self.line(h, move(4 - d)[0], what)
            self.done.append(self.copies.start(ref, ref, partner()))

    def close(self):
        self.done = []
        for h in range(2):
            self.close_half(h, self.rows, self.turned[h])
        for h in range(2):
            self.close_half(h, self.head, self.turned_head[h])

    def finish(self):
        for copy in self.done:
            copy.wait_recv()


class Reduce:
    def __init__(self, copies, sums, target_ref, base_ref, refs):
        self.copies, self.sums, self.target_ref, self.base_ref = copies, sums, target_ref, base_ref
        self.acc, self.in0, self.wire, self.part, self.in1, self.in2, self.zbuf, load_sem = refs
        p = position()[2]
        self.load = pltpu.make_async_copy(sums.at[:, :, p], self.acc, load_sem)
        self.load.start()

    def begin(self):
        p = position()[2]
        self.first = self.copies.start(self.sums.at[:, :, 1 - p], self.in0, partner())

    def pair(self):
        self.load.wait()
        self.first.wait_recv()
        acc, in0, wire = self.acc, self.in0, self.wire

        @pl.loop(0, 16)
        def _(i):
            a, b = i // 4, lax.rem(i, 4)
            total = acc[a, b] + in0[a, b]
            acc[a, b] = total
            if WIRE != F32:
                wire[a, b] = total.astype(WIRE)

        src = acc if WIRE == F32 else wire
        self.second = []
        for d in (2, 1, 3):
            to, peer = at_x(d)
            self.second.append(self.copies.start(src.at[to, :, :B], self.in1.at[0, d - 1], peer))
            to, peer = at_y(d)
            self.second.append(self.copies.start(src.at[:, to, B:], self.in1.at[1, d - 1], peer))

    def cross(self):
        x, y, _, _ = position()
        for copy in self.second:
            copy.wait_recv()
        acc, in1, part = self.acc, self.in1, self.part

        @pl.loop(0, 4)
        def _(i):
            part[0, i] = acc[x, i, :B] + (in1[0, 0, i].astype(F32) + in1[0, 1, i].astype(F32) + in1[0, 2, i].astype(F32))
            part[1, i] = acc[i, y, B:] + (in1[1, 0, i].astype(F32) + in1[1, 1, i].astype(F32) + in1[1, 2, i].astype(F32))

        self.third = []
        for d in (2, 1, 3):
            to, peer = at_y(d)
            self.third.append(self.copies.start(part.at[0, to], self.in2.at[0, d - 1], peer))
            to, peer = at_x(d)
            self.third.append(self.copies.start(part.at[1, to], self.in2.at[1, d - 1], peer))

    def finish(self):
        x, y, _, row = position()
        for copy in self.third:
            copy.wait_recv()
        part, in2, zbuf = self.part, self.in2, self.zbuf
        base = self.target_ref[:B] - (part[0, y] + in2[0, 0] + in2[0, 1] + in2[0, 2])
        self.base_ref[:B] = base
        zbuf[row] = base
        self.fourth = [self.copies.start(zbuf.at[row], zbuf.at[row], at_z(d)) for d in (2, 1, 3)]
        self.base_ref[B:] = self.target_ref[B:] - (part[1, x] + in2[1, 0] + in2[1, 1] + in2[1, 2])

    def diagonal(self, diag_ref, root):
        for copy in self.fourth:
            copy.wait_recv()
        diag_ref[...] = self.zbuf[root]


def step_kernel(step, last, *refs):
    refs = list(refs)
    take = lambda n: [refs.pop(0) for _ in range(n)]
    root_ref, parent_ref, sums, target_ref = take(4)
    low = take(1)[0] if step else None
    mine = None if last else take(1)[0]
    base_ref, diag_ref = take(2)
    out = take(1)[0] if step else None
    heads = None if last else take(1)[0]
    reduce_refs = take(8)
    headbuf = take(1)[0] if step else None
    send_sem, recv_sem = refs
    me, row = lax.axis_index("col"), lax.axis_index("row")
    copies = Copies(send_sem, recv_sem)
    reduce = Reduce(copies, sums, target_ref.at[step], base_ref, reduce_refs)
    if step:
        exchange = Exchange(copies, low, out, headbuf)
    greet([partner()] + [at_z(d) for d in (1, 2, 3)] + [f(d)[1] for f in (at_x, at_y) for d in (1, 2, 3)])
    if step:
        exchange.begin()
    reduce.begin()
    if not last:
        cast = Broadcast(copies, mine.at[step], heads)
    if step:
        exchange.pick(root_ref[step, parent_ref[step - 1, me]])
    reduce.pair()
    if step:
        exchange.turn()
    if not last:
        heads[row] = mine[step]
        cast.relay()
    reduce.cross()
    if step:
        exchange.close()
    reduce.finish()
    if step:
        exchange.finish()
    if not last:
        cast.finish()
    reduce.diagonal(diag_ref, root_ref[step, me])
    copies.finish()


def step_exchange(step, steps, roots, parent, sums, targets, low, chosen):
    rows, width = targets.shape[1:]
    last = step == steps - 1
    operands = [roots, parent, sums.reshape(4, 4, 2, rows, width), targets]
    in_specs = [SMEM, SMEM, ANY, VMEM]
    outs = [jax.ShapeDtypeStruct((rows, width), F32), jax.ShapeDtypeStruct((B, width), F32)]
    scratch = [
        pltpu.VMEM((4, 4, rows, width), F32),
        pltpu.VMEM((4, 4, rows, width), F32),
        pltpu.VMEM((4, 4, rows, width) if WIRE != F32 else (1, 1, 8, width), WIRE),
        pltpu.VMEM((2, 4, B, width), F32),
        pltpu.VMEM((2, 3, 4, B, width), WIRE),
        pltpu.VMEM((2, 3, B, width), F32),
        pltpu.VMEM((4, B, width), F32),
        pltpu.SemaphoreType.DMA,
    ]
    count = 16
    if step:
        operands.append(low.reshape(2, 2, H, width))
        in_specs.append(VMEM)
        outs.append(jax.ShapeDtypeStruct((2, 4, 4, 2, 3, H, width), BF16))
        scratch.append(pltpu.VMEM((4, 2, H, width), BF16))
        count += 43
    if not last:
        operands.append(chosen)
        in_specs.append(VMEM)
        outs.append(jax.ShapeDtypeStruct((4, 16, B, width), BF16))
        count += 6
    got = pl.pallas_call(
        functools.partial(step_kernel, step, last),
        out_shape=outs,
        in_specs=in_specs,
        out_specs=[VMEM] * len(outs),
        scratch_shapes=scratch + [pltpu.SemaphoreType.DMA((count,)), pltpu.SemaphoreType.DMA((count,))],
        compiler_params=pltpu.CompilerParams(collective_id=1 + step, has_side_effects=True),
        name=f"step_{step}",
    )(*operands)
    base, diag = got[:2]
    child = got[2].reshape(2, 32, 3, H, width) if step else jnp.zeros((2, 1, 3, 8, width), BF16)
    return base, diag, child, None if last else got[-1]


def local(targets, src_panels, live_counts, dest_owner, relative_map, diag_row, parent, chain_map):
    cols = lax.axis_size("col")
    steps, src = targets.shape[0], src_panels.shape[0]
    maps = relative_map.reshape(src, -1)
    chains = chain_map.reshape(steps - 1, -1)
    heads, chosen = open_heads(dest_owner, diag_row, src_panels, steps)
    out = low = None
    for s in range(steps):
        sums = slot_sums(s, live_counts, dest_owner, maps, src_panels, heads, cols)
        base, diag, child, heads = step_exchange(s, steps, diag_row, parent, sums, targets[:, 0], low, chosen)
        out, low = factor(s, steps, parent, chains, diag_row, base, diag, child, out)
    return out[:, None]


def solution(mesh):
    return jax.shard_map(
        local,
        mesh=mesh,
        in_specs=(
            P(None, "col", "row", None),
            P("col", "row", None),
            P("col"),
            P("col", None),
            P("col", None, "row"),
            P(),
            P(),
            P(None, None, "row"),
        ),
        out_specs=P(None, "col", "row", None),
        check_vma=False,
    )
```

```python
import functools

import jax
import jax.numpy as jnp
from jax import lax
from jax.experimental import pallas as pl
from jax.experimental.pallas import tpu as pltpu
from jax.sharding import PartitionSpec as P

F32 = jnp.float32
BF16 = jnp.bfloat16
B = 128
H = B // 2
TRANS_B = (((1,), (1,)), ((), ()))
TRANS_A = (((0,), (0,)), ((), ()))
MESH = pl.DeviceIdType.MESH
VMEM = pl.BlockSpec(memory_space=pltpu.VMEM)
SMEM = pl.BlockSpec(memory_space=pltpu.SMEM)
ANY = pl.BlockSpec(memory_space=pl.ANY)


def split_product(left, right):
    def parts(v):
        high = v.astype(BF16).astype(F32)
        mid = (v - high).astype(BF16).astype(F32)
        return high, mid, v - high - mid

    lh, lm, ll = parts(left)
    rh, rm, rl = parts(right)
    lefts = jnp.concatenate([lh, lh, lm, lh, ll, lm], axis=0).astype(BF16)
    rights = jnp.concatenate([rh, rm, rh, rl, rh, rm], axis=0).astype(BF16)
    return lax.dot_general(lefts, rights, TRANS_A, preferred_element_type=F32)


def cholesky_inverse(a, midway=None):
    n = a.shape[0]
    lane = lax.broadcasted_iota(jnp.int32, (8, n), 1)
    sub = lax.broadcasted_iota(jnp.int32, (8, n), 0)
    upper, inverse = [], []
    next_a, rest_a, next_w, rest_w = a[:8], a[8:], None, None
    for j in range(n // 8):
        if j == 10 and midway is not None:
            midway()
        pa = next_a
        pw = (lane == sub + 8 * j).astype(F32)
        if next_w is not None:
            pw = pw + next_w
        cols = [jnp.broadcast_to(pa[:, 8 * j + t : 8 * j + t + 1], (8, n)) for t in range(8)]
        pivots = jnp.zeros((8, n), F32)
        for t in range(8):
            d = jnp.broadcast_to(cols[t][t : t + 1], (8, n))
            pivots = jnp.where(sub == t, d, pivots)
            if t < 7:
                ratio = jnp.where(sub > t, cols[t] * (1.0 / d), 0.0)
                for v in range(t + 1, 8):
                    cols[v] = cols[v] - ratio * cols[v][t : t + 1]
                pa = pa - ratio * pa[t : t + 1]
                pw = pw - ratio * pw[t : t + 1]
        scale = lax.rsqrt(pivots)
        scale = scale * (1.5 - 0.5 * pivots * scale * scale)
        pa = jnp.where(lane >= sub + 8 * j, pa * scale, 0.0)
        pw = pw * scale
        upper.append(pa)
        inverse.append(pw)
        if j + 1 < n // 8:
            both = jnp.concatenate([pa, pw], axis=1)
            first = split_product(pa[:, 8 * j + 8 : 8 * j + 16], both)
            next_a = rest_a[:8] - first[:, :n]
            next_w = -first[:, n:] if rest_w is None else rest_w[:8] - first[:, n:]
            if j + 2 < n // 8:
                step = split_product(pa[:, 8 * j + 16 :], both)
                rest_a = rest_a[8:] - step[:, :n]
                rest_w = -step[:, n:] if rest_w is None else rest_w[8:] - step[:, n:]
    return jnp.concatenate(upper, axis=0).T, jnp.concatenate(inverse, axis=0)


def position():
    me = lax.axis_index("col")
    return me // 8, lax.rem(me // 2, 4), lax.rem(me, 2), lax.axis_index("row")


def at_x(d):
    x, y, p, _ = position()
    return lax.rem(x + d, 4), {"col": (lax.rem(x + d, 4) * 4 + y) * 2 + p}


def at_y(d):
    x, y, p, _ = position()
    return lax.rem(y + d, 4), {"col": (x * 4 + lax.rem(y + d, 4)) * 2 + p}


def at_z(d):
    return {"row": lax.rem(lax.axis_index("row") + d, 4)}


def partner():
    x, y, p, _ = position()
    return {"col": (x * 4 + y) * 2 + 1 - p}


def greet(peers):
    barrier = pltpu.get_barrier_semaphore()
    for peer in peers:
        pl.semaphore_signal(barrier, inc=1, device_id=peer, device_id_type=MESH)
    pl.semaphore_wait(barrier, len(peers))


class Copies:
    def __init__(self, send, recv):
        self.send, self.recv, self.count, self.open = send, recv, 0, []

    def start(self, src, dst, peer):
        n = self.count
        copy = pltpu.make_async_remote_copy(
            src_ref=src, dst_ref=dst, send_sem=self.send.at[n], recv_sem=self.recv.at[n], device_id=peer, device_id_type=MESH
        )
        copy.start()
        self.count += 1
        self.open.append(copy)
        return copy

    def sent(self, copies):
        for copy in copies:
            copy.wait_send()
        self.open = [copy for copy in self.open if all(copy is not other for other in copies)]

    def finish(self):
        self.sent(self.open)


class Broadcast:
    def __init__(self, copies, mine, out):
        row = lax.axis_index("row")
        self.copies, self.out = copies, out
        self.low, self.high = pl.ds(0, 8), pl.ds(8, 8)
        self.up = [copies.start(mine.at[part], out.at[row, part], at_z(1)) for part in (self.low, self.high)]
        self.down = [copies.start(mine.at[part], out.at[row, part], at_z(3)) for part in (self.high, self.low)]

    def relay(self):
        row = lax.axis_index("row")
        self.up[0].wait_recv()
        ref = self.out.at[lax.rem(row + 3, 4), self.low]
        self.on = [self.copies.start(ref, ref, at_z(1))]
        self.down[0].wait_recv()
        ref = self.out.at[lax.rem(row + 1, 4), self.high]
        self.on.append(self.copies.start(ref, ref, at_z(3)))

    def finish(self):
        for copy in [self.up[1], self.down[1]] + self.on:
            copy.wait_recv()


class Exchange:
    rows, head = slice(0, 2), slice(2, 3)

    def __init__(self, copies, low, out, zbuf):
        self.copies, self.out, self.zbuf = copies, out, zbuf
        x, y, p, row = position()
        for h in range(2):
            zbuf[row, h] = low[B + h * H : B + (h + 1) * H]
        for h in range(2):
            for b in range(2):
                out[h, x, y, p, b] = low[b * B + h * H : b * B + (h + 1) * H]

    def line(self, h, fixed, what):
        p = position()[2]
        return self.out.at[1, fixed, :, p, what] if h else self.out.at[0, :, fixed, p, what]

    def open_half(self, h, what, src):
        x, y, p, _ = position()
        move = at_y if h else at_x
        return [self.copies.start(src, self.out.at[h, x, y, p, what], move(d)[1]) for d in (2, 1, 3)]

    def begin(self):
        x, y, p, row = position()
        self.heads = [self.copies.start(self.zbuf.at[row], self.zbuf.at[row], at_z(d)) for d in (2, 1, 3)]
        self.opened = [self.open_half(h, self.rows, self.out.at[h, x, y, p, self.rows]) for h in range(2)]

    def pick(self, root):
        x, y, p, _ = position()
        for copy in self.heads:
            copy.wait_recv()
        picked = self.zbuf[root]
        for h in range(2):
            self.out[h, x, y, p, 2] = picked[h]
        self.opened_head = [self.open_half(h, self.head, self.out.at[h, x, y, p, self.head]) for h in range(2)]

    def turn_half(self, h, what, opened):
        x, y, _, _ = position()
        for copy in opened:
            copy.wait_recv()
        move, here = (at_x, x) if h else (at_y, y)
        ref = self.line(h, here, what)
        return [self.copies.start(ref, ref, move(d)[1]) for d in (2, 1, 3)], self.copies.start(ref, ref, partner())

    def turn(self):
        self.turned = [self.turn_half(h, self.rows, self.opened[h]) for h in range(2)]
        self.turned_head = [self.turn_half(h, self.head, self.opened_head[h]) for h in range(2)]

    def close_half(self, h, what, turned):
        self.done.append(turned[1])
        move = at_x if h else at_y
        for d, copy in zip((2, 1, 3), turned[0]):
            copy.wait_recv()
            ref = self.line(h, move(4 - d)[0], what)
            self.done.append(self.copies.start(ref, ref, partner()))

    def close(self):
        self.done = []
        for h in range(2):
            self.close_half(h, self.rows, self.turned[h])
        for h in range(2):
            self.close_half(h, self.head, self.turned_head[h])

    def finish(self):
        for copy in self.done:
            copy.wait_recv()


class Reduce:
    def __init__(self, copies, acc, away, in0, part, in1, in2, zbuf):
        self.copies, self.acc, self.away = copies, acc, away
        self.in0, self.part, self.in1, self.in2, self.zbuf = in0, part, in1, in2, zbuf

    def begin(self, previous, sums, slot):
        p = position()[2]
        if previous is not None:
            self.copies.sent([previous.first])
        self.own = lambda i: sums[slot(i * 2 + p)]

        @pl.loop(0, 16)
        def _(i):
            self.away[i // 4, lax.rem(i, 4)] = sums[slot(i * 2 + 1 - p)]

        self.first = self.copies.start(self.away, self.in0, partner())

    def pair(self, previous):
        if previous is not None:
            self.copies.sent(previous.second)
        self.first.wait_recv()
        acc, in0 = self.acc, self.in0

        @pl.loop(0, 16)
        def _(i):
            acc[i // 4, lax.rem(i, 4)] = self.own(i) + in0[i // 4, lax.rem(i, 4)]

        self.second = []
        for d in (2, 1, 3):
            to, peer = at_x(d)
            self.second.append(self.copies.start(acc.at[to, :, :B], self.in1.at[0, d - 1], peer))
            to, peer = at_y(d)
            self.second.append(self.copies.start(acc.at[:, to, B:], self.in1.at[1, d - 1], peer))

    def cross(self):
        x, y, _, _ = position()
        for copy in self.second:
            copy.wait_recv()
        acc, in1, part = self.acc, self.in1, self.part

        @pl.loop(0, 4)
        def _(i):
            part[0, i] = acc[x, i, :B] + (in1[0, 0, i] + in1[0, 1, i] + in1[0, 2, i])
            part[1, i] = acc[i, y, B:] + (in1[1, 0, i] + in1[1, 1, i] + in1[1, 2, i])

        self.third = []
        for d in (2, 1, 3):
            to, peer = at_y(d)
            self.third.append(self.copies.start(part.at[0, to], self.in2.at[0, d - 1], peer))
            to, peer = at_x(d)
            self.third.append(self.copies.start(part.at[1, to], self.in2.at[1, d - 1], peer))

    def finish(self, target, base):
        x, y, _, row = position()
        for copy in self.third:
            copy.wait_recv()
        part, in2, zbuf = self.part, self.in2, self.zbuf
        top = target[:B] - (part[0, y] + in2[0, 0] + in2[0, 1] + in2[0, 2])
        zbuf[row] = top
        base[:B] = top
        base[B:] = target[B:] - (part[1, x] + in2[1, 0] + in2[1, 1] + in2[1, 2])
        self.fourth = [self.copies.start(zbuf.at[row], zbuf.at[row], at_z(d)) for d in (2, 1, 3)]

    def diagonal(self, root):
        for copy in self.fourth:
            copy.wait_recv()
        return self.zbuf[root]


def window_kernel(
    dest_ref, map_ref, pred_ref, last_ref, root_ref, parent_ref, chain_ref, panel_hbm, target_ref, out_ref,
    panels, zb, chosen, heads, sums, away, acc, in0, part, in1, in2, upd, load_sem, send_sem, recv_sem, *bufs,
):
    steps = target_ref.shape[0]
    diags, child, headbuf = bufs[:steps], bufs[steps : 2 * steps - 1], bufs[2 * steps - 1 :]
    src = panels.shape[0]
    x, y, p, row = position()
    me = lax.axis_index("col")
    copies = Copies(send_sem, recv_sem)
    load = pltpu.make_async_copy(panel_hbm, panels, load_sem.at[0])

    def quarter(q):
        return panel_hbm.at[pl.ds(q * 16, 16), 0]

    own = pltpu.make_async_copy(quarter(row), zb.at[row], load_sem.at[1])
    own.start()
    sums[src] = jnp.zeros(sums.shape[1:], F32)
    greet([partner()] + [at_z(d) for d in (1, 2, 3)] + [f(d)[1] for f in (at_x, at_y) for d in (1, 2, 3)])
    opened = [copies.start(quarter(lax.rem(row + d, 4)), zb.at[row], at_z(d)) for d in (2, 1, 3)]
    load.start()
    own.wait()
    for copy in opened:
        copy.wait_recv()

    def choose(s):
        @pl.loop(0, 16)
        def _(j):
            chosen[s, j] = zb[root_ref[s, dest_ref[s, row * 16 + j]], j]

    def keep(s):
        @pl.loop(0, 16)
        def _(j):
            heads[s, row, j] = chosen[s, j]

    def products(s, quarters):
        @pl.loop(quarters[0] * 4, quarters[1] * 4)
        def _(g):
            prods = []
            for u in range(4):
                i = g * 4 + u
                first = map_ref[s, 0, i]
                block = jnp.concatenate([panels[i, first], panels[i, 1 - first]], axis=0)
                prods.append(
                    lax.dot_general(block, heads[s, i // 16, lax.rem(i, 16)], TRANS_B, preferred_element_type=F32)
                )
            for u in range(4):
                i = g * 4 + u
                sums[i] = prods[u] + sums[pred_ref[s, i]]

    reduces = [
        Reduce(copies, acc, away, in0.at[s], part.at[s], in1.at[s], in2.at[s], diags[s]) for s in range(steps)
    ]
    casts = {}

    def cast(s):
        casts[s] = Broadcast(copies, chosen.at[s], heads.at[s])

    def begin(s):
        reduces[s].begin(reduces[s - 1] if s else None, sums, lambda c: last_ref[s, c])

    def factor(s, midway):
        diag = reduces[s].diagonal(root_ref[s, me])
        upd[s, 2 * B :] = diag
        if s:

            @pl.loop(0, 16)
            def _(g):
                lefts, rights = [], []
                for u in range(2):
                    k = g * 2 + u
                    a, b, c = k // 8, lax.rem(k // 2, 4), u
                    chosen_child = parent_ref[s - 1, k] == me
                    head = jnp.concatenate([child[s - 1][h, a, b, c, 2] for h in range(2)], axis=0)
                    head = jnp.where(chosen_child, head, jnp.zeros_like(head))
                    first = chain_ref[s - 1, 0, k]
                    left_out = root_ref[s - 1, k] == row
                    blocks = []
                    for q in (first, 1 - first):
                        block = jnp.concatenate([child[s - 1][h, a, b, c, q] for h in range(2)], axis=0)
                        blocks.append(jnp.where(left_out & (q == 0), jnp.zeros_like(block), block))
                    lefts.append(jnp.concatenate(blocks + [head], axis=0))
                    rights.append(head)
                upd[s] -= lax.dot_general(
                    jnp.concatenate(lefts, axis=1), jnp.concatenate(rights, axis=1), TRANS_B, preferred_element_type=F32
                )

        lower, inverse = cholesky_inverse(upd[s, 2 * B :], midway)
        solved = lax.dot_general(
            upd[s, : 2 * B], inverse, TRANS_B, precision=lax.Precision.HIGHEST, preferred_element_type=F32
        )
        top = jnp.where(root_ref[s, me] == row, lower, solved[:B])
        panel = jnp.concatenate([top, solved[B:]], axis=0)
        out_ref[s] = panel
        return panel.astype(BF16)

    choose(0)
    cast(0)
    keep(0)
    for s in range(1, steps):
        choose(s)
        keep(s)
    casts[0].relay()
    cast(1)
    load.wait()
    casts[0].finish()
    products(0, (0, 4))
    begin(0)
    casts[1].relay()
    reduces[0].pair(None)
    casts[1].finish()
    products(1, (0, 4))
    begin(1)
    reduces[0].cross()
    reduces[1].pair(reduces[0])
    reduces[0].finish(target_ref.at[0], upd.at[0, : 2 * B])
    cast(2)
    low = factor(0, casts[2].relay)
    for s in range(steps - 1):
        ahead = s + 2 if s + 2 < steps else None
        exchange = Exchange(copies, low, child[s], headbuf[s])
        exchange.begin()
        reduces[s + 1].cross()
        exchange.pick(root_ref[s + 1, parent_ref[s, me]])
        if ahead:
            casts[ahead].finish()
            products(ahead, (0, 2))
        exchange.turn()
        if ahead:
            products(ahead, (2, 4))
            begin(ahead)
        reduces[s + 1].finish(target_ref.at[s + 1], upd.at[s + 1, : 2 * B])
        exchange.close()
        midway = None
        if s + 3 < steps:
            cast(s + 3)
            midway = casts[s + 3].relay
        if ahead:
            reduces[ahead].pair(reduces[ahead - 1])
        exchange.finish()
        low = factor(s + 1, midway)
    copies.finish()


def local(targets, src_panels, live_counts, dest_owner, relative_map, diag_row, parent, chain_map):
    steps, _, rows, width = targets.shape
    src = src_panels.shape[0]
    cols = lax.axis_size("col")
    dest = dest_owner.T
    index = jnp.arange(src)
    before = (dest[:, :, None] == dest[:, None, :]) & (index[None, :] < index[:, None])
    pred = jnp.max(jnp.where(before, index, -1), axis=2)
    pred = jnp.where(pred < 0, src, pred).astype(jnp.int32)
    mine = (dest[:, None, :] == jnp.arange(cols)[:, None]) & (index < live_counts[0])
    last = jnp.max(jnp.where(mine, index, -1), axis=2)
    last = jnp.where(last < 0, src, last).astype(jnp.int32)
    copies = 3 + steps * 22 + (steps - 1) * 43
    out = pl.pallas_call(
        window_kernel,
        out_shape=jax.ShapeDtypeStruct((steps, rows, width), F32),
        in_specs=[SMEM] * 7 + [ANY, VMEM],
        out_specs=VMEM,
        scratch_shapes=[
            pltpu.VMEM((src, 2, B, width), BF16),
            pltpu.VMEM((4, 16, B, width), BF16),
            pltpu.VMEM((steps, 16, B, width), BF16),
            pltpu.VMEM((steps, 4, 16, B, width), BF16),
            pltpu.VMEM((src + 1, rows, width), F32),
            pltpu.VMEM((4, 4, rows, width), F32),
            pltpu.VMEM((4, 4, rows, width), F32),
            pltpu.VMEM((steps, 4, 4, rows, width), F32),
            pltpu.VMEM((steps, 2, 4, B, width), F32),
            pltpu.VMEM((steps, 2, 3, 4, B, width), F32),
            pltpu.VMEM((steps, 2, 3, B, width), F32),
            pltpu.VMEM((steps, rows + B, width), F32),
            pltpu.SemaphoreType.DMA((2,)),
            pltpu.SemaphoreType.DMA((copies,)),
            pltpu.SemaphoreType.DMA((copies,)),
        ]
        + [pltpu.VMEM((4, B, width), F32)] * steps
        + [pltpu.VMEM((2, 4, 4, 2, 3, H, width), BF16)] * (steps - 1)
        + [pltpu.VMEM((4, 2, H, width), BF16)] * (steps - 1),
        compiler_params=pltpu.CompilerParams(collective_id=0, has_side_effects=True, vmem_limit_bytes=67_043_328),
        name="window",
    )(
        dest, relative_map.transpose(1, 2, 0), pred, last, diag_row, parent, chain_map.transpose(0, 2, 1),
        src_panels.reshape(src, 2, B, width), targets[:, 0],
    )
    return out[:, None]


def solution(mesh):
    return jax.shard_map(
        local,
        mesh=mesh,
        in_specs=(
            P(None, "col", "row", None),
            P("col", "row", None),
            P("col"),
            P("col", None),
            P("col", None, "row"),
            P(),
            P(),
            P(None, None, "row"),
        ),
        out_specs=P(None, "col", "row", None),
        check_vma=False,
    )
```

```python
import functools

import jax
import jax.numpy as jnp
from jax import lax
from jax.experimental import pallas as pl
from jax.experimental.pallas import tpu as pltpu
from jax.sharding import PartitionSpec as P

F32 = jnp.float32
BF16 = jnp.bfloat16
B = 128
H = B // 2
QUARTERS = (0, 1, 3, 2)
TRANS_B = (((1,), (1,)), ((), ()))
TRANS_A = (((0,), (0,)), ((), ()))
MESH = pl.DeviceIdType.MESH
VMEM = pl.BlockSpec(memory_space=pltpu.VMEM)
SMEM = pl.BlockSpec(memory_space=pltpu.SMEM)
ANY = pl.BlockSpec(memory_space=pl.ANY)


def split_product(left, right):
    def parts(v):
        high = v.astype(BF16).astype(F32)
        mid = (v - high).astype(BF16).astype(F32)
        return high, mid, v - high - mid

    lh, lm, ll = parts(left)
    rh, rm, rl = parts(right)
    lefts = jnp.concatenate([lh, lh, lm, lh, ll, lm], axis=0).astype(BF16)
    rights = jnp.concatenate([rh, rm, rh, rl, rh, rm], axis=0).astype(BF16)
    return lax.dot_general(lefts, rights, TRANS_A, preferred_element_type=F32)


def cholesky_inverse(a, midway=None):
    n, nb = a.shape[0], 16
    lane = lax.broadcasted_iota(jnp.int32, (nb, n), 1)
    sub = lax.broadcasted_iota(jnp.int32, (nb, n), 0)
    upper, inverse = [], []
    next_a, next_w = a, None
    for j in range(n // nb):
        if j == 2 and midway is not None:
            midway()
        pa, rest_a = next_a[:nb], next_a[nb:]
        pw = (lane == sub + nb * j).astype(F32)
        if next_w is not None:
            pw = pw + next_w[:nb]
        cols = [jnp.broadcast_to(pa[:, nb * j + t : nb * j + t + 1], (nb, n)) for t in range(nb)]
        pivots = jnp.zeros((nb, n), F32)
        for t in range(nb):
            d = jnp.broadcast_to(cols[t][t : t + 1], (8, n))
            pivots = jnp.where(sub == t, jnp.concatenate([d, d], axis=0), pivots)
            if t < nb - 1:
                r = 1.0 / d
                ratio = jnp.where(sub > t, cols[t] * jnp.concatenate([r, r], axis=0), 0.0)
                for v in range(t + 1, nb):
                    cols[v] = cols[v] - ratio * cols[v][t : t + 1]
                pa = pa - ratio * pa[t : t + 1]
                pw = pw - ratio * pw[t : t + 1]
        scale = lax.rsqrt(pivots)
        scale = scale * (1.5 - 0.5 * pivots * scale * scale)
        pa = jnp.where(lane >= sub + nb * j, pa * scale, 0.0)
        pw = pw * scale
        upper.append(pa)
        inverse.append(pw)
        if j + 1 < n // nb:
            step = split_product(pa[:, nb * j + nb :], jnp.concatenate([pa, pw], axis=1))
            next_a = rest_a - step[:, :n]
            next_w = -step[:, n:] if next_w is None else next_w[nb:] - step[:, n:]
    return jnp.concatenate(upper, axis=0).T, jnp.concatenate(inverse, axis=0)


def position():
    me = lax.axis_index("col")
    return me // 8, lax.rem(me // 2, 4), lax.rem(me, 2), lax.axis_index("row")


def at_x(d):
    x, y, p, _ = position()
    return lax.rem(x + d, 4), {"col": (lax.rem(x + d, 4) * 4 + y) * 2 + p}


def at_y(d):
    x, y, p, _ = position()
    return lax.rem(y + d, 4), {"col": (x * 4 + lax.rem(y + d, 4)) * 2 + p}


def at_z(d):
    return {"row": lax.rem(lax.axis_index("row") + d, 4)}


def partner():
    x, y, p, _ = position()
    return {"col": (x * 4 + y) * 2 + 1 - p}


def greet(peers):
    barrier = pltpu.get_barrier_semaphore()
    for peer in peers:
        pl.semaphore_signal(barrier, inc=1, device_id=peer, device_id_type=MESH)
    pl.semaphore_wait(barrier, len(peers))


class Copies:
    def __init__(self, send, recv):
        self.send, self.recv, self.count, self.open = send, recv, 0, []

    def start(self, src, dst, peer):
        n = self.count
        copy = pltpu.make_async_remote_copy(
            src_ref=src, dst_ref=dst, send_sem=self.send.at[n], recv_sem=self.recv.at[n], device_id=peer, device_id_type=MESH
        )
        copy.start()
        self.count += 1
        self.open.append(copy)
        return copy

    def sent(self, copies):
        for copy in copies:
            copy.wait_send()
        self.open = [copy for copy in self.open if all(copy is not other for other in copies)]

    def finish(self):
        self.sent(self.open)


class Broadcast:
    def __init__(self, copies, mine, out):
        self.copies, self.mine, self.out = copies, mine, out
        self.up, self.down, self.on = [], [], []

    def start(self, part):
        row = lax.axis_index("row")
        blocks = pl.ds(part * 8, 8)
        self.up.append(self.copies.start(self.mine.at[blocks], self.out.at[row, blocks], at_z(1)))
        self.down.append(self.copies.start(self.mine.at[blocks], self.out.at[row, blocks], at_z(3)))

    def relay(self, part):
        row = lax.axis_index("row")
        self.up[part].wait_recv()
        ref = self.out.at[lax.rem(row + 3, 4), pl.ds(part * 8, 4)]
        self.on.append(self.copies.start(ref, ref, at_z(1)))
        self.down[part].wait_recv()
        ref = self.out.at[lax.rem(row + 1, 4), pl.ds(part * 8 + 4, 4)]
        self.on.append(self.copies.start(ref, ref, at_z(3)))

    def finish(self):
        for copy in self.on:
            copy.wait_recv()


class Exchange:
    rows, head = slice(0, 2), slice(2, 3)

    def __init__(self, copies, low, out, zbuf):
        self.copies, self.out, self.zbuf = copies, out, zbuf
        x, y, p, row = position()
        for h in range(2):
            zbuf[row, h] = low[B + h * H : B + (h + 1) * H]
        for h in range(2):
            for b in range(2):
                out[h, x, y, p, b] = low[b * B + h * H : b * B + (h + 1) * H]

    def line(self, h, fixed, what):
        p = position()[2]
        return self.out.at[1, fixed, :, p, what] if h else self.out.at[0, :, fixed, p, what]

    def open_half(self, h, what, src):
        x, y, p, _ = position()
        move = at_y if h else at_x
        return [self.copies.start(src, self.out.at[h, x, y, p, what], move(d)[1]) for d in (2, 1, 3)]

    def begin(self):
        x, y, p, row = position()
        self.heads = [self.copies.start(self.zbuf.at[row], self.zbuf.at[row], at_z(d)) for d in (2, 1, 3)]
        self.opened = [self.open_half(h, self.rows, self.out.at[h, x, y, p, self.rows]) for h in range(2)]

    def pick(self, root):
        x, y, p, _ = position()
        for copy in self.heads:
            copy.wait_recv()
        picked = self.zbuf[root]
        for h in range(2):
            self.out[h, x, y, p, 2] = picked[h]
        self.opened_head = [self.open_half(h, self.head, self.out.at[h, x, y, p, self.head]) for h in range(2)]

    def turn_half(self, h, what, opened):
        x, y, _, _ = position()
        for copy in opened:
            copy.wait_recv()
        move, here = (at_x, x) if h else (at_y, y)
        ref = self.line(h, here, what)
        return [self.copies.start(ref, ref, move(d)[1]) for d in (2, 1, 3)], self.copies.start(ref, ref, partner())

    def turn(self):
        self.turned = [self.turn_half(h, self.rows, self.opened[h]) for h in range(2)]
        self.turned_head = [self.turn_half(h, self.head, self.opened_head[h]) for h in range(2)]

    def close_half(self, h, what, turned):
        self.done.append(turned[1])
        move = at_x if h else at_y
        for d, copy in zip((2, 1, 3), turned[0]):
            copy.wait_recv()
            ref = self.line(h, move(4 - d)[0], what)
            self.done.append(self.copies.start(ref, ref, partner()))

    def close_rows(self):
        self.done = []
        for h in range(2):
            self.close_half(h, self.rows, self.turned[h])

    def close_head(self):
        for h in range(2):
            self.close_half(h, self.head, self.turned_head[h])

    def finish(self):
        for copy in self.done:
            copy.wait_recv()


class Reduce:
    def __init__(self, copies, acc, away, in0, part, in1, in2, zbuf):
        self.copies, self.acc, self.away = copies, acc, away
        self.in0, self.part, self.in1, self.in2, self.zbuf = in0, part, in1, in2, zbuf

    def begin(self, previous, sums, slot):
        p = position()[2]
        if previous is not None:
            self.copies.sent(previous.first)
        self.own = lambda i: sums[slot(i * 2 + p)]
        self.first = []
        for d in (2, 1, 3, 0):
            to = at_x(d)[0]

            @pl.loop(0, 4)
            def _(i):
                self.away[to, i] = sums[slot((to * 4 + i) * 2 + 1 - p)]

            self.first.append(self.copies.start(self.away.at[to], self.in0.at[to], partner()))

    def pair(self, previous):
        if previous is not None:
            self.copies.sent(previous.second)
        acc, in0 = self.acc, self.in0
        self.second = []
        for d, first in zip((2, 1, 3, 0), self.first):
            to, peer = at_x(d)
            first.wait_recv()

            @pl.loop(0, 4)
            def _(i):
                acc[to, i] = self.own(to * 4 + i) + in0[to, i]

            if d:
                self.second.append(self.copies.start(acc.at[to, :, :B], self.in1.at[0, d - 1], peer))
        for d in (2, 1, 3):
            to, peer = at_y(d)
            self.second.append(self.copies.start(acc.at[:, to, B:], self.in1.at[1, d - 1], peer))

    def cross(self):
        x, y, _, _ = position()
        for copy in self.second:
            copy.wait_recv()
        acc, in1, part = self.acc, self.in1, self.part

        @pl.loop(0, 4)
        def _(i):
            part[0, i] = acc[x, i, :B] + (in1[0, 0, i] + in1[0, 1, i] + in1[0, 2, i])
            part[1, i] = acc[i, y, B:] + (in1[1, 0, i] + in1[1, 1, i] + in1[1, 2, i])

        self.third = []
        for d in (2, 1, 3):
            to, peer = at_y(d)
            self.third.append(self.copies.start(part.at[0, to], self.in2.at[0, d - 1], peer))
            to, peer = at_x(d)
            self.third.append(self.copies.start(part.at[1, to], self.in2.at[1, d - 1], peer))

    def finish(self, target, base):
        x, y, _, row = position()
        for copy in self.third:
            copy.wait_recv()
        part, in2, zbuf = self.part, self.in2, self.zbuf
        top = target[:B] - (part[0, y] + in2[0, 0] + in2[0, 1] + in2[0, 2])
        zbuf[row] = top
        base[:B] = top
        base[B:] = target[B:] - (part[1, x] + in2[1, 0] + in2[1, 1] + in2[1, 2])
        self.fourth = [self.copies.start(zbuf.at[row], zbuf.at[row], at_z(d)) for d in (2, 1, 3)]

    def diagonal(self, root):
        for copy in self.fourth:
            copy.wait_recv()
        return self.zbuf[root]


def window_kernel(
    dest_ref, map_ref, pred_ref, last_ref, root_ref, parent_ref, chain_ref, panel_hbm, target_ref, out_ref,
    panels, zb0, zb1, chosen, heads, sums, away, acc, in0, part, in1, in2, upd, load_sem, send_sem, recv_sem, *bufs,
):
    steps = target_ref.shape[0]
    diags, child, headbuf = bufs[:steps], bufs[steps : 2 * steps - 1], bufs[2 * steps - 1 :]
    src = panels.shape[0]
    x, y, p, row = position()
    me = lax.axis_index("col")
    copies = Copies(send_sem, recv_sem)
    load = pltpu.make_async_copy(panel_hbm, panels, load_sem.at[0])

    def quarter(q, part):
        return panel_hbm.at[pl.ds(q * 16 + part * 8, 8), 0]

    zb = (zb0, zb1)
    own = [pltpu.make_async_copy(quarter(row, i), zb[i].at[row], load_sem.at[1 + i]) for i in range(2)]
    for copy in own:
        copy.start()
    sums[src] = jnp.zeros(sums.shape[1:], F32)
    greet([partner()] + [at_z(d) for d in (1, 2, 3)] + [f(d)[1] for f in (at_x, at_y) for d in (1, 2, 3)])
    opened = [[copies.start(quarter(lax.rem(row + d, 4), i), zb[i].at[row], at_z(d)) for d in (2, 1, 3)] for i in range(2)]
    load.start()

    def choose(s, part):
        @pl.loop(0, 8)
        def _(j):
            i = part * 8 + j
            chosen[s, i] = zb[part][root_ref[s, dest_ref[s, row * 16 + i]], j]

    def keep(s):
        @pl.loop(0, 16)
        def _(j):
            heads[s, row, j] = chosen[s, j]

    def products(s, place):
        quarter = lax.rem(row + QUARTERS[place], 4)

        @pl.loop(0, 4)
        def _(g):
            prods = []
            for u in range(4):
                i = quarter * 16 + g * 4 + u
                first = map_ref[s, 0, i]
                block = jnp.concatenate([panels[i, first], panels[i, 1 - first]], axis=0)
                prods.append(
                    lax.dot_general(block, heads[s, quarter, g * 4 + u], TRANS_B, preferred_element_type=F32)
                )
            for u in range(4):
                i = quarter * 16 + g * 4 + u
                sums[place * 16 + g * 4 + u] = prods[u] + sums[pred_ref[s, i]]

    reduces = [
        Reduce(copies, acc, away, in0.at[s], part.at[s], in1.at[s], in2.at[s], diags[s]) for s in range(steps)
    ]
    casts = [Broadcast(copies, chosen.at[s], heads.at[s]) for s in range(steps)]

    def begin(s):
        reduces[s].begin(reduces[s - 1] if s else None, sums, lambda c: last_ref[s, c])

    def factor(s, midway):
        diag = reduces[s].diagonal(root_ref[s, me])
        upd[s, 2 * B :] = diag
        if s:

            @pl.loop(0, 16)
            def _(g):
                lefts, rights = [], []
                for u in range(2):
                    k = g * 2 + u
                    a, b, c = k // 8, lax.rem(k // 2, 4), u
                    chosen_child = parent_ref[s - 1, k] == me
                    head = jnp.concatenate([child[s - 1][h, a, b, c, 2] for h in range(2)], axis=0)
                    head = jnp.where(chosen_child, head, jnp.zeros_like(head))
                    first = chain_ref[s - 1, 0, k]
                    left_out = root_ref[s - 1, k] == row
                    blocks = []
                    for q in (first, 1 - first):
                        block = jnp.concatenate([child[s - 1][h, a, b, c, q] for h in range(2)], axis=0)
                        blocks.append(jnp.where(left_out & (q == 0), jnp.zeros_like(block), block))
                    lefts.append(jnp.concatenate(blocks + [head], axis=0))
                    rights.append(head)
                upd[s] -= lax.dot_general(
                    jnp.concatenate(lefts, axis=1), jnp.concatenate(rights, axis=1), TRANS_B, preferred_element_type=F32
                )

        lower, inverse = cholesky_inverse(upd[s, 2 * B :], midway)
        solved = lax.dot_general(
            upd[s, : 2 * B], inverse, TRANS_B, precision=lax.Precision.HIGHEST, preferred_element_type=F32
        )
        top = jnp.where(root_ref[s, me] == row, lower, solved[:B])
        panel = jnp.concatenate([top, solved[B:]], axis=0)
        out_ref[s] = panel
        return panel.astype(BF16)

    def both(action):
        for part in range(2):
            action(part)

    for part in range(2):
        own[part].wait()
        for copy in opened[part]:
            copy.wait_recv()
        choose(0, part)
        casts[0].start(part)
    keep(0)
    for s in range(1, steps):
        for part in range(2):
            choose(s, part)
        keep(s)
    load.wait()
    products(0, 0)
    both(casts[0].relay)
    both(casts[1].start)
    products(0, 1)
    products(0, 2)
    casts[0].finish()
    products(0, 3)
    begin(0)
    reduces[0].pair(None)
    both(casts[1].relay)
    for place in range(3):
        products(1, place)
    casts[1].finish()
    products(1, 3)
    begin(1)
    both(casts[2].start)
    reduces[0].cross()
    reduces[1].pair(reduces[0])
    reduces[0].finish(target_ref.at[0], upd.at[0, : 2 * B])
    both(casts[2].relay)
    low = factor(0, None)
    for s in range(steps - 1):
        ahead = s + 2 if s + 2 < steps else None
        exchange = Exchange(copies, low, child[s], headbuf[s])
        exchange.begin()
        exchange.pick(root_ref[s + 1, parent_ref[s, me]])
        reduces[s + 1].cross()
        if ahead:
            products(ahead, 0)
            products(ahead, 1)
        exchange.turn()
        if ahead:
            products(ahead, 2)
            casts[ahead].finish()
            products(ahead, 3)
            begin(ahead)
        reduces[s + 1].finish(target_ref.at[s + 1], upd.at[s + 1, : 2 * B])
        midway = None
        if s + 3 < steps:
            both(casts[s + 3].start)
            midway = functools.partial(both, casts[s + 3].relay)
        exchange.close_rows()
        if ahead:
            reduces[ahead].pair(reduces[ahead - 1])
        exchange.close_head()
        exchange.finish()
        low = factor(s + 1, midway)
    copies.finish()


def local(targets, src_panels, live_counts, dest_owner, relative_map, diag_row, parent, chain_map):
    steps, _, rows, width = targets.shape
    src = src_panels.shape[0]
    cols = lax.axis_size("col")
    dest = dest_owner.T
    index = jnp.arange(src)
    ahead = (index // 16 - lax.axis_index("row")) % 4
    rank = jnp.where(ahead < 2, ahead, 5 - ahead) * 16 + index % 16
    alive = index < live_counts[0]
    before = (dest[:, :, None] == dest[:, None, :]) & (rank[None, :] < rank[:, None]) & alive
    pred = jnp.max(jnp.where(before, rank, -1), axis=2)
    pred = jnp.where(pred < 0, src, pred).astype(jnp.int32)
    mine = (dest[:, None, :] == jnp.arange(cols)[:, None]) & alive
    last = jnp.max(jnp.where(mine, rank, -1), axis=2)
    last = jnp.where(last < 0, src, last).astype(jnp.int32)
    copies = 6 + steps * 27 + (steps - 1) * 43
    out = pl.pallas_call(
        window_kernel,
        out_shape=jax.ShapeDtypeStruct((steps, rows, width), F32),
        in_specs=[SMEM] * 7 + [ANY, VMEM],
        out_specs=VMEM,
        scratch_shapes=[
            pltpu.VMEM((src, 2, B, width), BF16),
            pltpu.VMEM((4, 8, B, width), BF16),
            pltpu.VMEM((4, 8, B, width), BF16),
            pltpu.VMEM((steps, 16, B, width), BF16),
            pltpu.VMEM((steps, 4, 16, B, width), BF16),
            pltpu.VMEM((src + 1, rows, width), F32),
            pltpu.VMEM((4, 4, rows, width), F32),
            pltpu.VMEM((4, 4, rows, width), F32),
            pltpu.VMEM((steps, 4, 4, rows, width), F32),
            pltpu.VMEM((steps, 2, 4, B, width), F32),
            pltpu.VMEM((steps, 2, 3, 4, B, width), F32),
            pltpu.VMEM((steps, 2, 3, B, width), F32),
            pltpu.VMEM((steps, rows + B, width), F32),
            pltpu.SemaphoreType.DMA((3,)),
            pltpu.SemaphoreType.DMA((copies,)),
            pltpu.SemaphoreType.DMA((copies,)),
        ]
        + [pltpu.VMEM((4, B, width), F32)] * steps
        + [pltpu.VMEM((2, 4, 4, 2, 3, H, width), BF16)] * (steps - 1)
        + [pltpu.VMEM((4, 2, H, width), BF16)] * (steps - 1),
        compiler_params=pltpu.CompilerParams(collective_id=0, has_side_effects=True, vmem_limit_bytes=67_043_328),
        name="window",
    )(
        dest, relative_map.transpose(1, 2, 0), pred, last, diag_row, parent, chain_map.transpose(0, 2, 1),
        src_panels.reshape(src, 2, B, width), targets[:, 0],
    )
    return out[:, None]


def solution(mesh):
    return jax.shard_map(
        local,
        mesh=mesh,
        in_specs=(
            P(None, "col", "row", None),
            P("col", "row", None),
            P("col"),
            P("col", None),
            P("col", None, "row"),
            P(),
            P(),
            P(None, None, "row"),
        ),
        out_specs=P(None, "col", "row", None),
        check_vma=False,
    )
```

```python
import functools

import jax
import jax.numpy as jnp
from jax import lax
from jax.experimental import pallas as pl
from jax.experimental.pallas import tpu as pltpu
from jax.sharding import PartitionSpec as P

F32 = jnp.float32
BF16 = jnp.bfloat16
B = 128
H = B // 2
QUARTERS = (0, 1, 3, 2)
TRANS_B = (((1,), (1,)), ((), ()))
TRANS_A = (((0,), (0,)), ((), ()))
MESH = pl.DeviceIdType.MESH
VMEM = pl.BlockSpec(memory_space=pltpu.VMEM)
SMEM = pl.BlockSpec(memory_space=pltpu.SMEM)
ANY = pl.BlockSpec(memory_space=pl.ANY)


def split_product(left, right):
    def parts(v):
        high = v.astype(BF16).astype(F32)
        mid = (v - high).astype(BF16).astype(F32)
        return high, mid, v - high - mid

    lh, lm, ll = parts(left)
    rh, rm, rl = parts(right)
    lefts = jnp.concatenate([lh, lh, lm, lh, ll, lm], axis=0).astype(BF16)
    rights = jnp.concatenate([rh, rm, rh, rl, rh, rm], axis=0).astype(BF16)
    return lax.dot_general(lefts, rights, TRANS_A, preferred_element_type=F32)


def cholesky_inverse(a):
    n, nb = a.shape[0], 16
    lane = lax.broadcasted_iota(jnp.int32, (nb, n), 1)
    sub = lax.broadcasted_iota(jnp.int32, (nb, n), 0)
    upper, inverse = [], []
    next_a, next_w = a, None
    for j in range(n // nb):
        pa, rest_a = next_a[:nb], next_a[nb:]
        pw = (lane == sub + nb * j).astype(F32)
        if next_w is not None:
            pw = pw + next_w[:nb]
        cols = [jnp.broadcast_to(pa[:, nb * j + t : nb * j + t + 1], (nb, n)) for t in range(nb)]
        pivots = jnp.zeros((nb, n), F32)
        for t in range(nb):
            d = jnp.broadcast_to(cols[t][t : t + 1], (8, n))
            pivots = jnp.where(sub == t, jnp.concatenate([d, d], axis=0), pivots)
            if t < nb - 1:
                r = 1.0 / d
                ratio = jnp.where(sub > t, cols[t] * jnp.concatenate([r, r], axis=0), 0.0)
                for v in range(t + 1, nb):
                    cols[v] = cols[v] - ratio * cols[v][t : t + 1]
                pa = pa - ratio * pa[t : t + 1]
                pw = pw - ratio * pw[t : t + 1]
        scale = lax.rsqrt(pivots)
        scale = scale * (1.5 - 0.5 * pivots * scale * scale)
        pa = jnp.where(lane >= sub + nb * j, pa * scale, 0.0)
        pw = pw * scale
        upper.append(pa)
        inverse.append(pw)
        if j + 1 < n // nb:
            step = split_product(pa[:, nb * j + nb :], jnp.concatenate([pa, pw], axis=1))
            next_a = rest_a - step[:, :n]
            next_w = -step[:, n:] if next_w is None else next_w[nb:] - step[:, n:]
    return jnp.concatenate(upper, axis=0).T, jnp.concatenate(inverse, axis=0)


def position():
    me = lax.axis_index("col")
    return me // 8, lax.rem(me // 2, 4), lax.rem(me, 2), lax.axis_index("row")


def at_x(d):
    x, y, p, _ = position()
    return lax.rem(x + d, 4), {"col": (lax.rem(x + d, 4) * 4 + y) * 2 + p}


def at_y(d):
    x, y, p, _ = position()
    return lax.rem(y + d, 4), {"col": (x * 4 + lax.rem(y + d, 4)) * 2 + p}


def at_z(d):
    return {"row": lax.rem(lax.axis_index("row") + d, 4)}


def partner():
    x, y, p, _ = position()
    return {"col": (x * 4 + y) * 2 + 1 - p}


def greet(peers):
    barrier = pltpu.get_barrier_semaphore()
    for peer in peers:
        pl.semaphore_signal(barrier, inc=1, device_id=peer, device_id_type=MESH)
    pl.semaphore_wait(barrier, len(peers))


class Copies:
    def __init__(self, send, recv):
        self.send, self.recv, self.count, self.open = send, recv, 0, []

    def start(self, src, dst, peer):
        n = self.count
        copy = pltpu.make_async_remote_copy(
            src_ref=src, dst_ref=dst, send_sem=self.send.at[n], recv_sem=self.recv.at[n], device_id=peer, device_id_type=MESH
        )
        copy.start()
        self.count += 1
        self.open.append(copy)
        return copy

    def sent(self, copies):
        for copy in copies:
            copy.wait_send()
        self.open = [copy for copy in self.open if all(copy is not other for other in copies)]

    def finish(self):
        self.sent(self.open)


class Broadcast:
    def __init__(self, copies, mine, out):
        self.copies, self.mine, self.out = copies, mine, out
        self.up, self.down, self.on = [], [], []

    def start(self, part):
        row = lax.axis_index("row")
        blocks = pl.ds(part * 8, 8)
        self.up.append(self.copies.start(self.mine.at[blocks], self.out.at[row, blocks], at_z(1)))
        self.down.append(self.copies.start(self.mine.at[blocks], self.out.at[row, blocks], at_z(3)))

    def relay(self, part):
        row = lax.axis_index("row")
        self.up[part].wait_recv()
        ref = self.out.at[lax.rem(row + 3, 4), pl.ds(part * 8, 4)]
        self.on.append(self.copies.start(ref, ref, at_z(1)))
        self.down[part].wait_recv()
        ref = self.out.at[lax.rem(row + 1, 4), pl.ds(part * 8 + 4, 4)]
        self.on.append(self.copies.start(ref, ref, at_z(3)))

    def finish(self):
        for copy in self.on:
            copy.wait_recv()


class Exchange:
    rows, head = slice(0, 2), slice(2, 3)

    def __init__(self, copies, low, out, zbuf):
        self.copies, self.out, self.zbuf = copies, out, zbuf
        x, y, p, row = position()
        for h in range(2):
            zbuf[row, h] = low[B + h * H : B + (h + 1) * H]
        for h in range(2):
            for b in range(2):
                out[h, x, y, p, b] = low[b * B + h * H : b * B + (h + 1) * H]

    def line(self, h, fixed, what):
        p = position()[2]
        return self.out.at[1, fixed, :, p, what] if h else self.out.at[0, :, fixed, p, what]

    def open_half(self, h, what, src):
        x, y, p, _ = position()
        move = at_y if h else at_x
        return [self.copies.start(src, self.out.at[h, x, y, p, what], move(d)[1]) for d in (2, 1, 3)]

    def begin(self):
        x, y, p, row = position()
        self.heads = [self.copies.start(self.zbuf.at[row], self.zbuf.at[row], at_z(d)) for d in (2, 1, 3)]
        self.opened = [self.open_half(h, self.rows, self.out.at[h, x, y, p, self.rows]) for h in range(2)]

    def pick(self, root):
        x, y, p, _ = position()
        for copy in self.heads:
            copy.wait_recv()
        picked = self.zbuf[root]
        for h in range(2):
            self.out[h, x, y, p, 2] = picked[h]
        self.opened_head = [self.open_half(h, self.head, self.out.at[h, x, y, p, self.head]) for h in range(2)]

    def turn_half(self, h, what, opened):
        x, y, _, _ = position()
        for copy in opened:
            copy.wait_recv()
        move, here = (at_x, x) if h else (at_y, y)
        ref = self.line(h, here, what)
        return [self.copies.start(ref, ref, move(d)[1]) for d in (2, 1, 3)], self.copies.start(ref, ref, partner())

    def turn(self):
        self.turned = [self.turn_half(h, self.rows, self.opened[h]) for h in range(2)]
        self.turned_head = [self.turn_half(h, self.head, self.opened_head[h]) for h in range(2)]

    def close_half(self, h, what, turned):
        self.done.append(turned[1])
        move = at_x if h else at_y
        for d, copy in zip((2, 1, 3), turned[0]):
            copy.wait_recv()
            ref = self.line(h, move(4 - d)[0], what)
            self.done.append(self.copies.start(ref, ref, partner()))

    def close_rows(self):
        self.done = []
        for h in range(2):
            self.close_half(h, self.rows, self.turned[h])

    def close_head(self):
        for h in range(2):
            self.close_half(h, self.head, self.turned_head[h])

    def finish(self):
        for copy in self.done:
            copy.wait_recv()


class Reduce:
    def __init__(self, copies, acc, away, in0, part, in1, in2, zbuf):
        self.copies, self.acc, self.away = copies, acc, away
        self.in0, self.part, self.in1, self.in2, self.zbuf = in0, part, in1, in2, zbuf

    def begin(self, previous, sums, slot):
        p = position()[2]
        if previous is not None:
            self.copies.sent(previous.first)
        self.own = lambda i: sums[slot(i * 2 + p)]
        self.first = []
        for d in (2, 1, 3, 0):
            to = at_x(d)[0]

            @pl.loop(0, 4)
            def _(i):
                self.away[to, i] = sums[slot((to * 4 + i) * 2 + 1 - p)]

            self.first.append(self.copies.start(self.away.at[to], self.in0.at[to], partner()))

    def pair(self, previous):
        if previous is not None:
            self.copies.sent(previous.second)
        acc, in0 = self.acc, self.in0
        self.second = []
        for d, first in zip((2, 1, 3, 0), self.first):
            to, peer = at_x(d)
            first.wait_recv()

            @pl.loop(0, 4)
            def _(i):
                acc[to, i] = self.own(to * 4 + i) + in0[to, i]

            if d:
                self.second.append(self.copies.start(acc.at[to, :, :B], self.in1.at[0, d - 1], peer))
        for d in (2, 1, 3):
            to, peer = at_y(d)
            self.second.append(self.copies.start(acc.at[:, to, B:], self.in1.at[1, d - 1], peer))

    def cross(self):
        x, y, _, _ = position()
        for copy in self.second:
            copy.wait_recv()
        acc, in1, part = self.acc, self.in1, self.part

        @pl.loop(0, 4)
        def _(i):
            part[0, i] = acc[x, i, :B] + (in1[0, 0, i] + in1[0, 1, i] + in1[0, 2, i])
            part[1, i] = acc[i, y, B:] + (in1[1, 0, i] + in1[1, 1, i] + in1[1, 2, i])

        self.third = []
        for d in (2, 1, 3):
            to, peer = at_y(d)
            self.third.append(self.copies.start(part.at[0, to], self.in2.at[0, d - 1], peer))
            to, peer = at_x(d)
            self.third.append(self.copies.start(part.at[1, to], self.in2.at[1, d - 1], peer))

    def finish(self, target, base):
        x, y, _, row = position()
        for copy in self.third:
            copy.wait_recv()
        part, in2, zbuf = self.part, self.in2, self.zbuf
        top = target[:B] - (part[0, y] + in2[0, 0] + in2[0, 1] + in2[0, 2])
        zbuf[row] = top
        base[:B] = top
        base[B:] = target[B:] - (part[1, x] + in2[1, 0] + in2[1, 1] + in2[1, 2])
        self.fourth = [self.copies.start(zbuf.at[row], zbuf.at[row], at_z(d)) for d in (2, 1, 3)]

    def diagonal(self, root):
        for copy in self.fourth:
            copy.wait_recv()
        return self.zbuf[root]


def window_kernel(
    dest_ref, map_ref, pred_ref, last_ref, root_ref, parent_ref, chain_ref, panel_hbm, target_ref, out_ref,
    panels, zb0, zb1, chosen, heads, sums, away, acc, in0, part, in1, in2, upd, load_sem, send_sem, recv_sem, *bufs,
):
    steps = target_ref.shape[0]
    diags, child, headbuf = bufs[:steps], bufs[steps : 2 * steps - 1], bufs[2 * steps - 1 :]
    src = panels.shape[0]
    x, y, p, row = position()
    me = lax.axis_index("col")
    copies = Copies(send_sem, recv_sem)
    load = pltpu.make_async_copy(panel_hbm, panels, load_sem.at[0])

    def quarter(q, part):
        return panel_hbm.at[pl.ds(q * 16 + part * 8, 8), 0]

    zb = (zb0, zb1)
    own = [pltpu.make_async_copy(quarter(row, i), zb[i].at[row], load_sem.at[1 + i]) for i in range(2)]
    for copy in own:
        copy.start()
    sums[src] = jnp.zeros(sums.shape[1:], F32)
    greet([partner()] + [at_z(d) for d in (1, 2, 3)] + [f(d)[1] for f in (at_x, at_y) for d in (1, 2, 3)])
    opened = [[copies.start(quarter(lax.rem(row + d, 4), i), zb[i].at[row], at_z(d)) for d in (2, 1, 3)] for i in range(2)]
    load.start()

    def choose(s, part):
        @pl.loop(0, 8)
        def _(j):
            i = part * 8 + j
            chosen[s, i] = zb[part][root_ref[s, dest_ref[s, row * 16 + i]], j]

    def keep(s):
        @pl.loop(0, 16)
        def _(j):
            heads[s, row, j] = chosen[s, j]

    def products(s, place):
        quarter = lax.rem(row + QUARTERS[place], 4)

        @pl.loop(0, 4)
        def _(g):
            prods = []
            for u in range(4):
                i = quarter * 16 + g * 4 + u
                first = map_ref[s, 0, i]
                block = jnp.concatenate([panels[i, first], panels[i, 1 - first]], axis=0)
                prods.append(
                    lax.dot_general(block, heads[s, quarter, g * 4 + u], TRANS_B, preferred_element_type=F32)
                )
            for u in range(4):
                i = quarter * 16 + g * 4 + u
                sums[place * 16 + g * 4 + u] = prods[u] + sums[pred_ref[s, i]]

    reduces = [
        Reduce(copies, acc, away, in0.at[s], part.at[s], in1.at[s], in2.at[s], diags[s]) for s in range(steps)
    ]
    casts = [Broadcast(copies, chosen.at[s], heads.at[s]) for s in range(steps)]

    def begin(s):
        reduces[s].begin(reduces[s - 1] if s else None, sums, lambda c: last_ref[s, c])

    def children(s, parity):
        @pl.loop(0, 8)
        def _(g):
            lefts, rights = [], []
            for u in range(2):
                a, b = g // 2, lax.rem(g, 2) * 2 + u
                k = (a * 4 + b) * 2 + parity
                mine = parent_ref[s - 1, k] == me
                head = jnp.concatenate([child[s - 1][h, a, b, parity, 2] for h in range(2)], axis=0)
                head = jnp.where(mine, head, jnp.zeros_like(head))
                first = chain_ref[s - 1, 0, k]
                left_out = root_ref[s - 1, k] == row
                blocks = [jnp.concatenate([child[s - 1][h, a, b, parity, q] for h in range(2)], axis=0) for q in range(2)]
                blocks[0] = jnp.where(left_out, jnp.zeros_like(blocks[0]), blocks[0])
                blocks = [jnp.where(first == q, blocks[0], blocks[1]) for q in range(2)]
                lefts.append(jnp.concatenate(blocks + [head], axis=0))
                rights.append(head)
            upd[s] -= lax.dot_general(
                jnp.concatenate(lefts, axis=1), jnp.concatenate(rights, axis=1), TRANS_B, preferred_element_type=F32
            )

    def factor(s):
        lower, inverse = cholesky_inverse(upd[s, 2 * B :])
        solved = lax.dot_general(
            upd[s, : 2 * B], inverse, TRANS_B, precision=lax.Precision.HIGHEST, preferred_element_type=F32
        )
        top = jnp.where(root_ref[s, me] == row, lower, solved[:B])
        panel = jnp.concatenate([top, solved[B:]], axis=0)
        out_ref[s] = panel
        return panel.astype(BF16)

    def both(action):
        for part in range(2):
            action(part)

    for part in range(2):
        own[part].wait()
        for copy in opened[part]:
            copy.wait_recv()
        choose(0, part)
        casts[0].start(part)
    keep(0)
    for s in range(1, steps):
        for part in range(2):
            choose(s, part)
        keep(s)
    load.wait()
    products(0, 0)
    both(casts[0].relay)
    both(casts[1].start)
    products(0, 1)
    products(0, 2)
    casts[0].finish()
    products(0, 3)
    begin(0)
    reduces[0].pair(None)
    both(casts[1].relay)
    casts[2].start(0)
    for place in range(3):
        products(1, place)
    casts[1].finish()
    products(1, 3)
    begin(1)
    reduces[0].cross()
    reduces[1].pair(reduces[0])
    casts[2].relay(0)
    reduces[0].finish(target_ref.at[0], upd.at[0, : 2 * B])
    casts[2].start(1)
    upd[0, 2 * B :] = reduces[0].diagonal(root_ref[0, me])
    low = factor(0)
    for s in range(steps - 1):
        ahead = s + 2 if s + 2 < steps else None
        exchange = Exchange(copies, low, child[s], headbuf[s])
        exchange.begin()
        exchange.pick(root_ref[s + 1, parent_ref[s, me]])
        if ahead:
            casts[ahead].relay(1)
        if s + 3 < steps:
            casts[s + 3].start(0)
        reduces[s + 1].cross()
        if ahead:
            products(ahead, 0)
            products(ahead, 1)
        exchange.turn()
        if ahead:
            products(ahead, 2)
            casts[ahead].finish()
            products(ahead, 3)
            begin(ahead)
        reduces[s + 1].finish(target_ref.at[s + 1], upd.at[s + 1, : 2 * B])
        if s + 3 < steps:
            casts[s + 3].relay(0)
            casts[s + 3].start(1)
        if ahead:
            reduces[ahead].pair(reduces[ahead - 1])
        exchange.close_rows()
        exchange.close_head()
        upd[s + 1, 2 * B :] = reduces[s + 1].diagonal(root_ref[s + 1, me])
        children(s + 1, p)
        exchange.finish()
        children(s + 1, 1 - p)
        low = factor(s + 1)
    copies.finish()


def local(targets, src_panels, live_counts, dest_owner, relative_map, diag_row, parent, chain_map):
    steps, _, rows, width = targets.shape
    src = src_panels.shape[0]
    cols = lax.axis_size("col")
    dest = dest_owner.T
    index = jnp.arange(src)
    ahead = (index // 16 - lax.axis_index("row")) % 4
    rank = jnp.where(ahead < 2, ahead, 5 - ahead) * 16 + index % 16
    alive = index < live_counts[0]
    before = (dest[:, :, None] == dest[:, None, :]) & (rank[None, :] < rank[:, None]) & alive
    pred = jnp.max(jnp.where(before, rank, -1), axis=2)
    pred = jnp.where(pred < 0, src, pred).astype(jnp.int32)
    mine = (dest[:, None, :] == jnp.arange(cols)[:, None]) & alive
    last = jnp.max(jnp.where(mine, rank, -1), axis=2)
    last = jnp.where(last < 0, src, last).astype(jnp.int32)
    copies = 6 + steps * 27 + (steps - 1) * 43
    out = pl.pallas_call(
        window_kernel,
        out_shape=jax.ShapeDtypeStruct((steps, rows, width), F32),
        in_specs=[SMEM] * 7 + [ANY, VMEM],
        out_specs=VMEM,
        scratch_shapes=[
            pltpu.VMEM((src, 2, B, width), BF16),
            pltpu.VMEM((4, 8, B, width), BF16),
            pltpu.VMEM((4, 8, B, width), BF16),
            pltpu.VMEM((steps, 16, B, width), BF16),
            pltpu.VMEM((steps, 4, 16, B, width), BF16),
            pltpu.VMEM((src + 1, rows, width), F32),
            pltpu.VMEM((4, 4, rows, width), F32),
            pltpu.VMEM((4, 4, rows, width), F32),
            pltpu.VMEM((steps, 4, 4, rows, width), F32),
            pltpu.VMEM((steps, 2, 4, B, width), F32),
            pltpu.VMEM((steps, 2, 3, 4, B, width), F32),
            pltpu.VMEM((steps, 2, 3, B, width), F32),
            pltpu.VMEM((steps, rows + B, width), F32),
            pltpu.SemaphoreType.DMA((3,)),
            pltpu.SemaphoreType.DMA((copies,)),
            pltpu.SemaphoreType.DMA((copies,)),
        ]
        + [pltpu.VMEM((4, B, width), F32)] * steps
        + [pltpu.VMEM((2, 4, 4, 2, 3, H, width), BF16)] * (steps - 1)
        + [pltpu.VMEM((4, 2, H, width), BF16)] * (steps - 1),
        compiler_params=pltpu.CompilerParams(collective_id=0, has_side_effects=True, vmem_limit_bytes=67_043_328),
        name="window",
    )(
        dest, relative_map.transpose(1, 2, 0), pred, last, diag_row, parent, chain_map.transpose(0, 2, 1),
        src_panels.reshape(src, 2, B, width), targets[:, 0],
    )
    return out[:, None]


def solution(mesh):
    return jax.shard_map(
        local,
        mesh=mesh,
        in_specs=(
            P(None, "col", "row", None),
            P("col", "row", None),
            P("col"),
            P("col", None),
            P("col", None, "row"),
            P(),
            P(),
            P(None, None, "row"),
        ),
        out_specs=P(None, "col", "row", None),
        check_vma=False,
    )
```

```python
import functools

import jax
import jax.numpy as jnp
from jax import lax
from jax.experimental import pallas as pl
from jax.experimental.pallas import tpu as pltpu
from jax.sharding import PartitionSpec as P

F32 = jnp.float32
BF16 = jnp.bfloat16
B = 128
H = B // 2
QUARTERS = (0, 1, 3, 2)
TRANS_B = (((1,), (1,)), ((), ()))
TRANS_A = (((0,), (0,)), ((), ()))
MESH = pl.DeviceIdType.MESH
VMEM = pl.BlockSpec(memory_space=pltpu.VMEM)
SMEM = pl.BlockSpec(memory_space=pltpu.SMEM)
ANY = pl.BlockSpec(memory_space=pl.ANY)


def split_product(left, right):
    def parts(v):
        high = v.astype(BF16).astype(F32)
        mid = (v - high).astype(BF16).astype(F32)
        return high, mid, v - high - mid

    lh, lm, ll = parts(left)
    rh, rm, rl = parts(right)
    lefts = jnp.concatenate([lh, lh, lm, lh, ll, lm], axis=0).astype(BF16)
    rights = jnp.concatenate([rh, rm, rh, rl, rh, rm], axis=0).astype(BF16)
    return lax.dot_general(lefts, rights, TRANS_A, preferred_element_type=F32)


def cholesky_inverse(a):
    n, nb = a.shape[0], 16
    lane = lax.broadcasted_iota(jnp.int32, (nb, n), 1)
    sub = lax.broadcasted_iota(jnp.int32, (nb, n), 0)
    upper, inverse = [], []
    next_a, next_w = a, None
    for j in range(n // nb):
        pa, rest_a = next_a[:nb], next_a[nb:]
        pw = (lane == sub + nb * j).astype(F32)
        if next_w is not None:
            pw = pw + next_w[:nb]
        cols = [jnp.broadcast_to(pa[:, nb * j + t : nb * j + t + 1], (nb, n)) for t in range(nb)]
        pivots = jnp.zeros((nb, n), F32)
        for t in range(nb):
            d = jnp.broadcast_to(cols[t][t : t + 1], (8, n))
            pivots = jnp.where(sub == t, jnp.concatenate([d, d], axis=0), pivots)
            if t < nb - 1:
                r = 1.0 / d
                ratio = jnp.where(sub > t, cols[t] * jnp.concatenate([r, r], axis=0), 0.0)
                for v in range(t + 1, nb):
                    cols[v] = cols[v] - ratio * cols[v][t : t + 1]
                pa = pa - ratio * pa[t : t + 1]
                pw = pw - ratio * pw[t : t + 1]
        scale = lax.rsqrt(pivots)
        scale = scale * (1.5 - 0.5 * pivots * scale * scale)
        pa = jnp.where(lane >= sub + nb * j, pa * scale, 0.0)
        pw = pw * scale
        upper.append(pa)
        inverse.append(pw)
        if j + 1 < n // nb:
            step = split_product(pa[:, nb * j + nb :], jnp.concatenate([pa, pw], axis=1))
            next_a = rest_a - step[:, :n]
            next_w = -step[:, n:] if next_w is None else next_w[nb:] - step[:, n:]
    return jnp.concatenate(upper, axis=0).T, jnp.concatenate(inverse, axis=0)


def position():
    me = lax.axis_index("col")
    return me // 8, lax.rem(me // 2, 4), lax.rem(me, 2), lax.axis_index("row")


def at_x(d):
    x, y, p, _ = position()
    return lax.rem(x + d, 4), {"col": (lax.rem(x + d, 4) * 4 + y) * 2 + p}


def at_y(d):
    x, y, p, _ = position()
    return lax.rem(y + d, 4), {"col": (x * 4 + lax.rem(y + d, 4)) * 2 + p}


def at_z(d):
    return {"row": lax.rem(lax.axis_index("row") + d, 4)}


def partner():
    x, y, p, _ = position()
    return {"col": (x * 4 + y) * 2 + 1 - p}


def greet(peers):
    barrier = pltpu.get_barrier_semaphore()
    for peer in peers:
        pl.semaphore_signal(barrier, inc=1, device_id=peer, device_id_type=MESH)
    pl.semaphore_wait(barrier, len(peers))


class Copies:
    def __init__(self, send, recv):
        self.send, self.recv, self.count, self.open = send, recv, 0, []

    def start(self, src, dst, peer):
        n = self.count
        copy = pltpu.make_async_remote_copy(
            src_ref=src, dst_ref=dst, send_sem=self.send.at[n], recv_sem=self.recv.at[n], device_id=peer, device_id_type=MESH
        )
        copy.start()
        self.count += 1
        self.open.append(copy)
        return copy

    def sent(self, copies):
        for copy in copies:
            copy.wait_send()
        self.open = [copy for copy in self.open if all(copy is not other for other in copies)]

    def finish(self):
        self.sent(self.open)


class Broadcast:
    def __init__(self, copies, mine, out):
        self.copies, self.mine, self.out = copies, mine, out
        self.up, self.down, self.on = [], [], []

    def start(self, part):
        row = lax.axis_index("row")
        blocks = pl.ds(part * 8, 8)
        self.up.append(self.copies.start(self.mine.at[blocks], self.out.at[row, blocks], at_z(1)))
        self.down.append(self.copies.start(self.mine.at[blocks], self.out.at[row, blocks], at_z(3)))

    def relay(self, part):
        row = lax.axis_index("row")
        self.up[part].wait_recv()
        ref = self.out.at[lax.rem(row + 3, 4), pl.ds(part * 8, 4)]
        self.on.append(self.copies.start(ref, ref, at_z(1)))
        self.down[part].wait_recv()
        ref = self.out.at[lax.rem(row + 1, 4), pl.ds(part * 8 + 4, 4)]
        self.on.append(self.copies.start(ref, ref, at_z(3)))

    def finish(self):
        for copy in self.on:
            copy.wait_recv()


class Exchange:
    rows, head = slice(0, 2), slice(2, 3)

    def __init__(self, copies, low, out, zbuf):
        self.copies, self.out, self.zbuf = copies, out, zbuf
        x, y, p, row = position()
        for h in range(2):
            zbuf[row, h] = low[B + h * H : B + (h + 1) * H]
        for h in range(2):
            for b in range(2):
                out[h, x, y, p, b] = low[b * B + h * H : b * B + (h + 1) * H]

    def line(self, h, fixed, what):
        p = position()[2]
        return self.out.at[1, fixed, :, p, what] if h else self.out.at[0, :, fixed, p, what]

    def open_half(self, h, what, src):
        x, y, p, _ = position()
        move = at_y if h else at_x
        return [self.copies.start(src, self.out.at[h, x, y, p, what], move(d)[1]) for d in (2, 1, 3)]

    def begin(self):
        x, y, p, row = position()
        self.heads = [self.copies.start(self.zbuf.at[row], self.zbuf.at[row], at_z(d)) for d in (2, 1, 3)]
        self.opened = [self.open_half(h, self.rows, self.out.at[h, x, y, p, self.rows]) for h in range(2)]

    def pick(self, root):
        x, y, p, _ = position()
        for copy in self.heads:
            copy.wait_recv()
        picked = self.zbuf[root]
        for h in range(2):
            self.out[h, x, y, p, 2] = picked[h]
        self.opened_head = [self.open_half(h, self.head, self.out.at[h, x, y, p, self.head]) for h in range(2)]

    def turn_half(self, h, what, opened):
        x, y, _, _ = position()
        for copy in opened:
            copy.wait_recv()
        move, here = (at_x, x) if h else (at_y, y)
        ref = self.line(h, here, what)
        return [self.copies.start(ref, ref, move(d)[1]) for d in (2, 1, 3)], self.copies.start(ref, ref, partner())

    def turn(self):
        self.turned = [self.turn_half(h, self.rows, self.opened[h]) for h in range(2)]
        self.turned_head = [self.turn_half(h, self.head, self.opened_head[h]) for h in range(2)]

    def close_half(self, h, what, turned):
        self.done.append(turned[1])
        move = at_x if h else at_y
        for d, copy in zip((2, 1, 3), turned[0]):
            copy.wait_recv()
            ref = self.line(h, move(4 - d)[0], what)
            self.done.append(self.copies.start(ref, ref, partner()))

    def close_rows(self):
        self.done = []
        for h in range(2):
            self.close_half(h, self.rows, self.turned[h])

    def close_head(self):
        for h in range(2):
            self.close_half(h, self.head, self.turned_head[h])

    def finish(self):
        for copy in self.done:
            copy.wait_recv()


class Reduce:
    def __init__(self, copies, acc, away, in0, part, far, in1, in2, zbuf):
        self.copies, self.acc, self.away, self.far = copies, acc, away, far
        self.in0, self.part, self.in1, self.in2, self.zbuf = in0, part, in1, in2, zbuf

    def begin(self, previous, sums, slot):
        p = position()[2]
        if previous is not None:
            self.copies.sent(previous.first)
        self.own = lambda i: sums[slot(i * 2 + p)]
        self.first = []
        for d in (2, 1, 3, 0):
            to = at_x(d)[0]

            @pl.loop(0, 4)
            def _(i):
                self.away[to, i] = sums[slot((to * 4 + i) * 2 + 1 - p)]

            self.first.append(self.copies.start(self.away.at[to], self.in0.at[to], partner()))

    def pair(self, previous):
        if previous is not None:
            self.copies.sent(previous.opened + previous.second)
        acc, in0, far = self.acc, self.in0, self.far
        self.opened = []
        for d, first in zip((2, 1, 3, 0), self.first):
            to = at_x(d)[0]
            first.wait_recv()

            @pl.loop(0, 4)
            def _(i):
                acc[to, i] = self.own(to * 4 + i) + in0[to, i]

            if d == 2:
                self.opened.append(self.copies.start(acc.at[to, :2, :B], far.at[0, 0], at_x(1)[1]))
                self.opened.append(self.copies.start(acc.at[to, 2:, :B], far.at[0, 1], at_x(3)[1]))
        to = at_y(2)[0]
        self.opened.append(self.copies.start(acc.at[:2, to, B:], far.at[1, 0], at_y(1)[1]))
        self.opened.append(self.copies.start(acc.at[2:, to, B:], far.at[1, 1], at_y(3)[1]))

    def combine(self):
        for copy in self.opened:
            copy.wait_recv()
        acc, far, in1 = self.acc, self.far, self.in1
        self.second = []
        for n, d in enumerate((1, 3)):
            (to_x, peer_x), (to_y, peer_y) = at_x(d), at_y(d)
            for i in range(2):
                acc[to_x, 2 * n + i, :B] += far[0, n, i]
                acc[2 * n + i, to_y, B:] += far[1, n, i]
            self.second.append(self.copies.start(acc.at[to_x, :, :B], in1.at[0, n], peer_x))
            self.second.append(self.copies.start(acc.at[:, to_y, B:], in1.at[1, n], peer_y))

    def cross(self):
        x, y, _, _ = position()
        for copy in self.second:
            copy.wait_recv()
        acc, in1, part = self.acc, self.in1, self.part

        @pl.loop(0, 4)
        def _(i):
            part[0, i] = acc[x, i, :B] + (in1[0, 0, i] + in1[0, 1, i])
            part[1, i] = acc[i, y, B:] + (in1[1, 0, i] + in1[1, 1, i])

        self.third = []
        for d in (2, 1, 3):
            to, peer = at_y(d)
            self.third.append(self.copies.start(part.at[0, to], self.in2.at[0, d - 1], peer))
            to, peer = at_x(d)
            self.third.append(self.copies.start(part.at[1, to], self.in2.at[1, d - 1], peer))

    def finish(self, target, base):
        x, y, _, row = position()
        for copy in self.third:
            copy.wait_recv()
        part, in2, zbuf = self.part, self.in2, self.zbuf
        top = target[:B] - (part[0, y] + in2[0, 0] + in2[0, 1] + in2[0, 2])
        zbuf[row] = top
        base[:B] = top
        base[B:] = target[B:] - (part[1, x] + in2[1, 0] + in2[1, 1] + in2[1, 2])
        self.fourth = [self.copies.start(zbuf.at[row], zbuf.at[row], at_z(d)) for d in (2, 1, 3)]

    def diagonal(self, root):
        for copy in self.fourth:
            copy.wait_recv()
        return self.zbuf[root]


def window_kernel(
    dest_ref, map_ref, pred_ref, last_ref, root_ref, parent_ref, chain_ref, panel_hbm, target_ref, out_ref,
    panels, zb0, zb1, chosen, heads, sums, away, acc, in0, part, far, in1, in2, upd, load_sem, send_sem, recv_sem, *bufs,
):
    steps = target_ref.shape[0]
    diags, child, headbuf = bufs[:steps], bufs[steps : 2 * steps - 1], bufs[2 * steps - 1 :]
    src = panels.shape[0]
    x, y, p, row = position()
    me = lax.axis_index("col")
    copies = Copies(send_sem, recv_sem)
    load = pltpu.make_async_copy(panel_hbm, panels, load_sem.at[0])

    def quarter(q, part):
        return panel_hbm.at[pl.ds(q * 16 + part * 8, 8), 0]

    zb = (zb0, zb1)
    own = [pltpu.make_async_copy(quarter(row, i), zb[i].at[row], load_sem.at[1 + i]) for i in range(2)]
    for copy in own:
        copy.start()
    sums[src] = jnp.zeros(sums.shape[1:], F32)
    greet([partner()] + [at_z(d) for d in (1, 2, 3)] + [f(d)[1] for f in (at_x, at_y) for d in (1, 2, 3)])
    opened = [[copies.start(quarter(lax.rem(row + d, 4), i), zb[i].at[row], at_z(d)) for d in (2, 1, 3)] for i in range(2)]
    load.start()

    def choose(s, part):
        @pl.loop(0, 8)
        def _(j):
            i = part * 8 + j
            chosen[s, i] = zb[part][root_ref[s, dest_ref[s, row * 16 + i]], j]

    def keep(s):
        @pl.loop(0, 16)
        def _(j):
            heads[s, row, j] = chosen[s, j]

    def products(s, place):
        quarter = lax.rem(row + QUARTERS[place], 4)

        @pl.loop(0, 4)
        def _(g):
            prods = []
            for u in range(4):
                i = quarter * 16 + g * 4 + u
                first = map_ref[s, 0, i]
                block = jnp.concatenate([panels[i, first], panels[i, 1 - first]], axis=0)
                prods.append(
                    lax.dot_general(block, heads[s, quarter, g * 4 + u], TRANS_B, preferred_element_type=F32)
                )
            for u in range(4):
                i = quarter * 16 + g * 4 + u
                sums[place * 16 + g * 4 + u] = prods[u] + sums[pred_ref[s, i]]

    reduces = [
        Reduce(copies, acc, away, in0.at[s], part.at[s], far.at[s], in1.at[s], in2.at[s], diags[s]) for s in range(steps)
    ]
    casts = [Broadcast(copies, chosen.at[s], heads.at[s]) for s in range(steps)]

    def begin(s):
        reduces[s].begin(reduces[s - 1] if s else None, sums, lambda c: last_ref[s, c])

    def children(s, parity):
        @pl.loop(0, 8)
        def _(g):
            lefts, rights = [], []
            for u in range(2):
                a, b = g // 2, lax.rem(g, 2) * 2 + u
                k = (a * 4 + b) * 2 + parity
                mine = parent_ref[s - 1, k] == me
                head = jnp.concatenate([child[s - 1][h, a, b, parity, 2] for h in range(2)], axis=0)
                head = jnp.where(mine, head, jnp.zeros_like(head))
                first = chain_ref[s - 1, 0, k]
                left_out = root_ref[s - 1, k] == row
                blocks = [jnp.concatenate([child[s - 1][h, a, b, parity, q] for h in range(2)], axis=0) for q in range(2)]
                blocks[0] = jnp.where(left_out, jnp.zeros_like(blocks[0]), blocks[0])
                blocks = [jnp.where(first == q, blocks[0], blocks[1]) for q in range(2)]
                lefts.append(jnp.concatenate(blocks + [head], axis=0))
                rights.append(head)
            upd[s] -= lax.dot_general(
                jnp.concatenate(lefts, axis=1), jnp.concatenate(rights, axis=1), TRANS_B, preferred_element_type=F32
            )

    def factor(s):
        lower, inverse = cholesky_inverse(upd[s, 2 * B :])
        solved = lax.dot_general(
            upd[s, : 2 * B], inverse, TRANS_B, precision=lax.Precision.HIGHEST, preferred_element_type=F32
        )
        top = jnp.where(root_ref[s, me] == row, lower, solved[:B])
        panel = jnp.concatenate([top, solved[B:]], axis=0)
        out_ref[s] = panel
        return panel.astype(BF16)

    def both(action):
        for part in range(2):
            action(part)

    for part in range(2):
        own[part].wait()
        for copy in opened[part]:
            copy.wait_recv()
        choose(0, part)
        casts[0].start(part)
    keep(0)
    for s in range(1, steps):
        for part in range(2):
            choose(s, part)
        keep(s)
    load.wait()
    products(0, 0)
    both(casts[0].relay)
    both(casts[1].start)
    products(0, 1)
    products(0, 2)
    casts[0].finish()
    products(0, 3)
    begin(0)
    reduces[0].pair(None)
    casts[1].relay(0)
    reduces[0].combine()
    casts[1].relay(1)
    casts[2].start(0)
    for place in range(3):
        products(1, place)
    casts[1].finish()
    products(1, 3)
    begin(1)
    reduces[0].cross()
    reduces[1].pair(reduces[0])
    casts[2].relay(0)
    reduces[0].finish(target_ref.at[0], upd.at[0, : 2 * B])
    casts[2].start(1)
    reduces[1].combine()
    upd[0, 2 * B :] = reduces[0].diagonal(root_ref[0, me])
    low = factor(0)
    for s in range(steps - 1):
        ahead = s + 2 if s + 2 < steps else None
        exchange = Exchange(copies, low, child[s], headbuf[s])
        exchange.begin()
        exchange.pick(root_ref[s + 1, parent_ref[s, me]])
        if ahead:
            casts[ahead].relay(1)
        if s + 3 < steps:
            casts[s + 3].start(0)
        reduces[s + 1].cross()
        if ahead:
            products(ahead, 0)
            products(ahead, 1)
        exchange.turn()
        if ahead:
            products(ahead, 2)
            casts[ahead].finish()
            products(ahead, 3)
            begin(ahead)
        reduces[s + 1].finish(target_ref.at[s + 1], upd.at[s + 1, : 2 * B])
        if s + 3 < steps:
            casts[s + 3].relay(0)
            casts[s + 3].start(1)
        if ahead:
            reduces[ahead].pair(reduces[ahead - 1])
        exchange.close_rows()
        exchange.close_head()
        upd[s + 1, 2 * B :] = reduces[s + 1].diagonal(root_ref[s + 1, me])
        if ahead:
            reduces[ahead].combine()
        children(s + 1, p)
        exchange.finish()
        children(s + 1, 1 - p)
        low = factor(s + 1)
    copies.finish()


def local(targets, src_panels, live_counts, dest_owner, relative_map, diag_row, parent, chain_map):
    steps, _, rows, width = targets.shape
    src = src_panels.shape[0]
    cols = lax.axis_size("col")
    dest = dest_owner.T
    index = jnp.arange(src)
    ahead = (index // 16 - lax.axis_index("row")) % 4
    rank = jnp.where(ahead < 2, ahead, 5 - ahead) * 16 + index % 16
    alive = index < live_counts[0]
    before = (dest[:, :, None] == dest[:, None, :]) & (rank[None, :] < rank[:, None]) & alive
    pred = jnp.max(jnp.where(before, rank, -1), axis=2)
    pred = jnp.where(pred < 0, src, pred).astype(jnp.int32)
    mine = (dest[:, None, :] == jnp.arange(cols)[:, None]) & alive
    last = jnp.max(jnp.where(mine, rank, -1), axis=2)
    last = jnp.where(last < 0, src, last).astype(jnp.int32)
    copies = 6 + steps * 29 + (steps - 1) * 43
    out = pl.pallas_call(
        window_kernel,
        out_shape=jax.ShapeDtypeStruct((steps, rows, width), F32),
        in_specs=[SMEM] * 7 + [ANY, VMEM],
        out_specs=VMEM,
        scratch_shapes=[
            pltpu.VMEM((src, 2, B, width), BF16),
            pltpu.VMEM((4, 8, B, width), BF16),
            pltpu.VMEM((4, 8, B, width), BF16),
            pltpu.VMEM((steps, 16, B, width), BF16),
            pltpu.VMEM((steps, 4, 16, B, width), BF16),
            pltpu.VMEM((src + 1, rows, width), F32),
            pltpu.VMEM((4, 4, rows, width), F32),
            pltpu.VMEM((4, 4, rows, width), F32),
            pltpu.VMEM((steps, 4, 4, rows, width), F32),
            pltpu.VMEM((steps, 2, 4, B, width), F32),
            pltpu.VMEM((steps, 2, 2, 2, B, width), F32),
            pltpu.VMEM((steps, 2, 2, 4, B, width), F32),
            pltpu.VMEM((steps, 2, 3, B, width), F32),
            pltpu.VMEM((steps, rows + B, width), F32),
            pltpu.SemaphoreType.DMA((3,)),
            pltpu.SemaphoreType.DMA((copies,)),
            pltpu.SemaphoreType.DMA((copies,)),
        ]
        + [pltpu.VMEM((4, B, width), F32)] * steps
        + [pltpu.VMEM((2, 4, 4, 2, 3, H, width), BF16)] * (steps - 1)
        + [pltpu.VMEM((4, 2, H, width), BF16)] * (steps - 1),
        compiler_params=pltpu.CompilerParams(collective_id=0, has_side_effects=True, vmem_limit_bytes=67_043_328),
        name="window",
    )(
        dest, relative_map.transpose(1, 2, 0), pred, last, diag_row, parent, chain_map.transpose(0, 2, 1),
        src_panels.reshape(src, 2, B, width), targets[:, 0],
    )
    return out[:, None]


def solution(mesh):
    return jax.shard_map(
        local,
        mesh=mesh,
        in_specs=(
            P(None, "col", "row", None),
            P("col", "row", None),
            P("col"),
            P("col", None),
            P("col", None, "row"),
            P(),
            P(),
            P(None, None, "row"),
        ),
        out_specs=P(None, "col", "row", None),
        check_vma=False,
    )
```

```python
import functools

import jax
import jax.numpy as jnp
from jax import lax
from jax.experimental import pallas as pl
from jax.experimental.pallas import tpu as pltpu
from jax.sharding import PartitionSpec as P

F32 = jnp.float32
BF16 = jnp.bfloat16
B = 128
H = B // 2
QUARTERS = (0, 1, 3, 2)
TRANS_B = (((1,), (1,)), ((), ()))
TRANS_A = (((0,), (0,)), ((), ()))
MESH = pl.DeviceIdType.MESH
VMEM = pl.BlockSpec(memory_space=pltpu.VMEM)
SMEM = pl.BlockSpec(memory_space=pltpu.SMEM)
ANY = pl.BlockSpec(memory_space=pl.ANY)


def split_product(left, right):
    def parts(v):
        high = v.astype(BF16).astype(F32)
        mid = (v - high).astype(BF16).astype(F32)
        return high, mid, v - high - mid

    lh, lm, ll = parts(left)
    rh, rm, rl = parts(right)
    lefts = jnp.concatenate([lh, lh, lm, lh, ll, lm], axis=0).astype(BF16)
    rights = jnp.concatenate([rh, rm, rh, rl, rh, rm], axis=0).astype(BF16)
    return lax.dot_general(lefts, rights, TRANS_A, preferred_element_type=F32)


def cholesky_inverse(a):
    n, nb = a.shape[0], 16
    lane = lax.broadcasted_iota(jnp.int32, (nb, n), 1)
    sub = lax.broadcasted_iota(jnp.int32, (nb, n), 0)
    upper, inverse = [], []
    next_a, next_w = a, None
    for j in range(n // nb):
        pa, rest_a = next_a[:nb], next_a[nb:]
        pw = (lane == sub + nb * j).astype(F32)
        if next_w is not None:
            pw = pw + next_w[:nb]
        cols = [jnp.broadcast_to(pa[:, nb * j + t : nb * j + t + 1], (nb, n)) for t in range(nb)]
        pivots = jnp.zeros((nb, n), F32)
        for t in range(nb):
            d = jnp.broadcast_to(cols[t][t : t + 1], (8, n))
            pivots = jnp.where(sub == t, jnp.concatenate([d, d], axis=0), pivots)
            if t < nb - 1:
                r = 1.0 / d
                ratio = jnp.where(sub > t, cols[t] * jnp.concatenate([r, r], axis=0), 0.0)
                for v in range(t + 1, nb):
                    cols[v] = cols[v] - ratio * cols[v][t : t + 1]
                pa = pa - ratio * pa[t : t + 1]
                pw = pw - ratio * pw[t : t + 1]
        scale = lax.rsqrt(pivots)
        scale = scale * (1.5 - 0.5 * pivots * scale * scale)
        pa = jnp.where(lane >= sub + nb * j, pa * scale, 0.0)
        pw = pw * scale
        upper.append(pa)
        inverse.append(pw)
        if j + 1 < n // nb:
            step = split_product(pa[:, nb * j + nb :], jnp.concatenate([pa, pw], axis=1))
            next_a = rest_a - step[:, :n]
            next_w = -step[:, n:] if next_w is None else next_w[nb:] - step[:, n:]
    return jnp.concatenate(upper, axis=0).T, jnp.concatenate(inverse, axis=0)


def position():
    me = lax.axis_index("col")
    return me // 8, lax.rem(me // 2, 4), lax.rem(me, 2), lax.axis_index("row")


def at_x(d):
    x, y, p, _ = position()
    return lax.rem(x + d, 4), {"col": (lax.rem(x + d, 4) * 4 + y) * 2 + p}


def at_y(d):
    x, y, p, _ = position()
    return lax.rem(y + d, 4), {"col": (x * 4 + lax.rem(y + d, 4)) * 2 + p}


def at_z(d):
    return {"row": lax.rem(lax.axis_index("row") + d, 4)}


def partner():
    x, y, p, _ = position()
    return {"col": (x * 4 + y) * 2 + 1 - p}


def greet(peers):
    barrier = pltpu.get_barrier_semaphore()
    for peer in peers:
        pl.semaphore_signal(barrier, inc=1, device_id=peer, device_id_type=MESH)
    pl.semaphore_wait(barrier, len(peers))


class Copies:
    def __init__(self, send, recv):
        self.send, self.recv, self.count, self.open = send, recv, 0, []

    def start(self, src, dst, peer):
        n = self.count
        copy = pltpu.make_async_remote_copy(
            src_ref=src, dst_ref=dst, send_sem=self.send.at[n], recv_sem=self.recv.at[n], device_id=peer, device_id_type=MESH
        )
        copy.start()
        self.count += 1
        self.open.append(copy)
        return copy

    def sent(self, copies):
        for copy in copies:
            copy.wait_send()
        self.open = [copy for copy in self.open if all(copy is not other for other in copies)]

    def finish(self):
        self.sent(self.open)


class Broadcast:
    def __init__(self, copies, mine, out):
        self.copies, self.mine, self.out = copies, mine, out
        self.up, self.down, self.on = [], [], []

    def start(self, part):
        row = lax.axis_index("row")
        blocks = pl.ds(part * 8, 8)
        self.up.append(self.copies.start(self.mine.at[blocks], self.out.at[row, blocks], at_z(1)))
        self.down.append(self.copies.start(self.mine.at[blocks], self.out.at[row, blocks], at_z(3)))

    def relay(self, part):
        row = lax.axis_index("row")
        self.up[part].wait_recv()
        ref = self.out.at[lax.rem(row + 3, 4), pl.ds(part * 8, 4)]
        self.on.append(self.copies.start(ref, ref, at_z(1)))
        self.down[part].wait_recv()
        ref = self.out.at[lax.rem(row + 1, 4), pl.ds(part * 8 + 4, 4)]
        self.on.append(self.copies.start(ref, ref, at_z(3)))

    def finish(self):
        for copy in self.on:
            copy.wait_recv()


class Exchange:
    rows, head = slice(0, 2), slice(2, 3)

    def __init__(self, copies, low, out, zbuf):
        self.copies, self.out, self.zbuf = copies, out, zbuf
        x, y, p, row = position()
        for h in range(2):
            zbuf[row, h] = low[B + h * H : B + (h + 1) * H]
        for h in range(2):
            for b in range(2):
                out[h, x, y, p, b] = low[b * B + h * H : b * B + (h + 1) * H]

    def line(self, h, fixed, what):
        p = position()[2]
        return self.out.at[1, fixed, :, p, what] if h else self.out.at[0, :, fixed, p, what]

    def open_half(self, h, what, src):
        x, y, p, _ = position()
        move = at_y if h else at_x
        return [self.copies.start(src, self.out.at[h, x, y, p, what], move(d)[1]) for d in (2, 1, 3)]

    def begin(self):
        x, y, p, row = position()
        self.heads = [self.copies.start(self.zbuf.at[row], self.zbuf.at[row], at_z(d)) for d in (2, 1, 3)]
        self.opened = [self.open_half(h, self.rows, self.out.at[h, x, y, p, self.rows]) for h in range(2)]

    def pick(self, root):
        x, y, p, _ = position()
        for copy in self.heads:
            copy.wait_recv()
        picked = self.zbuf[root]
        for h in range(2):
            self.out[h, x, y, p, 2] = picked[h]
        self.opened_head = [self.open_half(h, self.head, self.out.at[h, x, y, p, self.head]) for h in range(2)]

    def turn_half(self, h, what, opened):
        x, y, _, _ = position()
        for copy in opened:
            copy.wait_recv()
        move, here = (at_x, x) if h else (at_y, y)
        ref = self.line(h, here, what)
        return [self.copies.start(ref, ref, move(d)[1]) for d in (2, 1, 3)], self.copies.start(ref, ref, partner())

    def turn(self):
        self.turned = [self.turn_half(h, self.rows, self.opened[h]) for h in range(2)]
        self.turned_head = [self.turn_half(h, self.head, self.opened_head[h]) for h in range(2)]

    def close_half(self, h, what, turned):
        self.done.append(turned[1])
        move = at_x if h else at_y
        for d, copy in zip((2, 1, 3), turned[0]):
            copy.wait_recv()
            ref = self.line(h, move(4 - d)[0], what)
            self.done.append(self.copies.start(ref, ref, partner()))

    def close_rows(self):
        self.done = []
        for h in range(2):
            self.close_half(h, self.rows, self.turned[h])

    def close_head(self):
        for h in range(2):
            self.close_half(h, self.head, self.turned_head[h])

    def finish(self):
        for copy in self.done:
            copy.wait_recv()


class Reduce:
    def __init__(self, copies, acc, away, in0, part, far, in1, in2, zbuf):
        self.copies, self.acc, self.away, self.far = copies, acc, away, far
        self.in0, self.part, self.in1, self.in2, self.zbuf = in0, part, in1, in2, zbuf

    def begin(self, previous, sums, slot):
        p = position()[2]
        if previous is not None:
            self.copies.sent(previous.first)
        self.own = lambda i: sums[slot(i * 2 + p)]
        self.first = []
        for d in (2, 1, 3, 0):
            to = at_x(d)[0]

            @pl.loop(0, 4)
            def _(i):
                self.away[to, i] = sums[slot((to * 4 + i) * 2 + 1 - p)]

            self.first.append(self.copies.start(self.away.at[to], self.in0.at[to], partner()))

    def pair(self, previous):
        if previous is not None:
            self.copies.sent(previous.opened + previous.second)
        acc, in0, far = self.acc, self.in0, self.far
        self.opened = []
        for d, first in zip((2, 1, 3, 0), self.first):
            to = at_x(d)[0]
            first.wait_recv()

            @pl.loop(0, 4)
            def _(i):
                acc[to, i] = self.own(to * 4 + i) + in0[to, i]

            if d == 2:
                self.opened.append(self.copies.start(acc.at[to, :2, :B], far.at[0, 0], at_x(1)[1]))
                self.opened.append(self.copies.start(acc.at[to, 2:, :B], far.at[0, 1], at_x(3)[1]))
        to = at_y(2)[0]
        self.opened.append(self.copies.start(acc.at[:2, to, B:], far.at[1, 0], at_y(1)[1]))
        self.opened.append(self.copies.start(acc.at[2:, to, B:], far.at[1, 1], at_y(3)[1]))

    def combine(self):
        for copy in self.opened:
            copy.wait_recv()
        acc, far, in1 = self.acc, self.far, self.in1
        self.second = []
        for n, d in enumerate((1, 3)):
            (to_x, peer_x), (to_y, peer_y) = at_x(d), at_y(d)
            for i in range(2):
                acc[to_x, 2 * n + i, :B] += far[0, n, i]
                acc[2 * n + i, to_y, B:] += far[1, n, i]
            self.second.append(self.copies.start(acc.at[to_x, :, :B], in1.at[0, n], peer_x))
            self.second.append(self.copies.start(acc.at[:, to_y, B:], in1.at[1, n], peer_y))

    def cross(self):
        x, y, _, _ = position()
        for copy in self.second:
            copy.wait_recv()
        acc, in1, part = self.acc, self.in1, self.part

        @pl.loop(0, 4)
        def _(i):
            part[0, i] = acc[x, i, :B] + (in1[0, 0, i] + in1[0, 1, i])
            part[1, i] = acc[i, y, B:] + (in1[1, 0, i] + in1[1, 1, i])

        self.third = []
        for d in (2, 1, 3):
            to, peer = at_y(d)
            self.third.append(self.copies.start(part.at[0, to], self.in2.at[0, d - 1], peer))
            to, peer = at_x(d)
            self.third.append(self.copies.start(part.at[1, to], self.in2.at[1, d - 1], peer))

    def finish(self, target, base):
        x, y, _, row = position()
        for copy in self.third:
            copy.wait_recv()
        part, in2, zbuf = self.part, self.in2, self.zbuf
        top = target[:B] - (part[0, y] + in2[0, 0] + in2[0, 1] + in2[0, 2])
        zbuf[row] = top
        base[:B] = top
        base[B:] = target[B:] - (part[1, x] + in2[1, 0] + in2[1, 1] + in2[1, 2])
        self.fourth = [self.copies.start(zbuf.at[row], zbuf.at[row], at_z(d)) for d in (2, 1, 3)]

    def diagonal(self, root):
        for copy in self.fourth:
            copy.wait_recv()
        return self.zbuf[root]


def window_kernel(
    dest_hbm, map_hbm, pred_hbm, last_hbm, root_hbm, parent_hbm, chain_hbm, panel_hbm, target_hbm, out_ref,
    dest_ref, map_ref, pred_ref, last_ref, root_ref, parent_ref, chain_ref, target_ref,
    panels, zb0, zb1, chosen, heads, sums, away, acc, in0, part, far, in1, in2, upd, load_sem, send_sem, recv_sem, *bufs,
):
    steps = target_ref.shape[0]
    diags, child, headbuf = bufs[:steps], bufs[steps : 2 * steps - 1], bufs[2 * steps - 1 :]
    src = panels.shape[0]
    x, y, p, row = position()
    me = lax.axis_index("col")
    copies = Copies(send_sem, recv_sem)
    load = pltpu.make_async_copy(panel_hbm, panels, load_sem.at[0])

    def quarter(q, part):
        return panel_hbm.at[pl.ds(q * 16 + part * 8, 8), 0]

    tables = [
        pltpu.make_async_copy(a, b, load_sem.at[3 + n])
        for n, (a, b) in enumerate(
            (
                (dest_hbm, dest_ref), (map_hbm, map_ref), (pred_hbm, pred_ref), (last_hbm, last_ref),
                (root_hbm, root_ref), (parent_hbm, parent_ref), (chain_hbm, chain_ref), (target_hbm, target_ref),
            )
        )
    ]
    zb = (zb0, zb1)
    own = [pltpu.make_async_copy(quarter(row, i), zb[i].at[row], load_sem.at[1 + i]) for i in range(2)]
    for copy in own:
        copy.start()
    sums[src] = jnp.zeros(sums.shape[1:], F32)
    greet([partner()] + [at_z(d) for d in (1, 2, 3)] + [f(d)[1] for f in (at_x, at_y) for d in (1, 2, 3)])
    opened = [[copies.start(quarter(lax.rem(row + d, 4), i), zb[i].at[row], at_z(d)) for d in (2, 1, 3)] for i in range(2)]
    for table in tables:
        table.start()
    load.start()
    for table in tables:
        table.wait()

    def choose(s, part):
        @pl.loop(0, 8)
        def _(j):
            i = part * 8 + j
            chosen[s, i] = zb[part][root_ref[s, dest_ref[s, row * 16 + i]], j]

    def keep(s):
        @pl.loop(0, 16)
        def _(j):
            heads[s, row, j] = chosen[s, j]

    def products(s, place):
        quarter = lax.rem(row + QUARTERS[place], 4)

        @pl.loop(0, 4)
        def _(g):
            prods = []
            for u in range(4):
                i = quarter * 16 + g * 4 + u
                first = map_ref[s, 0, i]
                block = jnp.concatenate([panels[i, first], panels[i, 1 - first]], axis=0)
                prods.append(
                    lax.dot_general(block, heads[s, quarter, g * 4 + u], TRANS_B, preferred_element_type=F32)
                )
            for u in range(4):
                i = quarter * 16 + g * 4 + u
                sums[place * 16 + g * 4 + u] = prods[u] + sums[pred_ref[s, i]]

    reduces = [
        Reduce(copies, acc, away, in0.at[s], part.at[s], far.at[s], in1.at[s], in2.at[s], diags[s]) for s in range(steps)
    ]
    casts = [Broadcast(copies, chosen.at[s], heads.at[s]) for s in range(steps)]

    def begin(s):
        reduces[s].begin(reduces[s - 1] if s else None, sums, lambda c: last_ref[s, c])

    def children(s, parity):
        @pl.loop(0, 8)
        def _(g):
            lefts, rights = [], []
            for u in range(2):
                a, b = g // 2, lax.rem(g, 2) * 2 + u
                k = (a * 4 + b) * 2 + parity
                mine = parent_ref[s - 1, k] == me
                head = jnp.concatenate([child[s - 1][h, a, b, parity, 2] for h in range(2)], axis=0)
                head = jnp.where(mine, head, jnp.zeros_like(head))
                first = chain_ref[s - 1, 0, k]
                left_out = root_ref[s - 1, k] == row
                blocks = [jnp.concatenate([child[s - 1][h, a, b, parity, q] for h in range(2)], axis=0) for q in range(2)]
                blocks[0] = jnp.where(left_out, jnp.zeros_like(blocks[0]), blocks[0])
                blocks = [jnp.where(first == q, blocks[0], blocks[1]) for q in range(2)]
                lefts.append(jnp.concatenate(blocks + [head], axis=0))
                rights.append(head)
            upd[s] -= lax.dot_general(
                jnp.concatenate(lefts, axis=1), jnp.concatenate(rights, axis=1), TRANS_B, preferred_element_type=F32
            )

    def factor(s):
        lower, inverse = cholesky_inverse(upd[s, 2 * B :])
        solved = lax.dot_general(
            upd[s, : 2 * B], inverse, TRANS_B, precision=lax.Precision.HIGHEST, preferred_element_type=F32
        )
        top = jnp.where(root_ref[s, me] == row, lower, solved[:B])
        panel = jnp.concatenate([top, solved[B:]], axis=0)
        out_ref[s] = panel
        return panel.astype(BF16)

    def both(action):
        for part in range(2):
            action(part)

    for part in range(2):
        own[part].wait()
        for copy in opened[part]:
            copy.wait_recv()
        choose(0, part)
        casts[0].start(part)
    keep(0)
    for s in range(1, steps):
        for part in range(2):
            choose(s, part)
        keep(s)
    load.wait()
    products(0, 0)
    both(casts[0].relay)
    both(casts[1].start)
    products(0, 1)
    products(0, 2)
    casts[0].finish()
    products(0, 3)
    begin(0)
    reduces[0].pair(None)
    casts[1].relay(0)
    reduces[0].combine()
    casts[1].relay(1)
    casts[2].start(0)
    for place in range(3):
        products(1, place)
    casts[1].finish()
    products(1, 3)
    begin(1)
    reduces[0].cross()
    reduces[1].pair(reduces[0])
    casts[2].relay(0)
    reduces[0].finish(target_ref.at[0], upd.at[0, : 2 * B])
    casts[2].start(1)
    reduces[1].combine()
    upd[0, 2 * B :] = reduces[0].diagonal(root_ref[0, me])
    low = factor(0)
    for s in range(steps - 1):
        ahead = s + 2 if s + 2 < steps else None
        exchange = Exchange(copies, low, child[s], headbuf[s])
        exchange.begin()
        exchange.pick(root_ref[s + 1, parent_ref[s, me]])
        if ahead:
            casts[ahead].relay(1)
        if s + 3 < steps:
            casts[s + 3].start(0)
        reduces[s + 1].cross()
        if ahead:
            products(ahead, 0)
            products(ahead, 1)
        exchange.turn()
        if ahead:
            products(ahead, 2)
            casts[ahead].finish()
            products(ahead, 3)
            begin(ahead)
        reduces[s + 1].finish(target_ref.at[s + 1], upd.at[s + 1, : 2 * B])
        if s + 3 < steps:
            casts[s + 3].relay(0)
            casts[s + 3].start(1)
        if ahead:
            reduces[ahead].pair(reduces[ahead - 1])
        exchange.close_rows()
        exchange.close_head()
        upd[s + 1, 2 * B :] = reduces[s + 1].diagonal(root_ref[s + 1, me])
        if ahead:
            reduces[ahead].combine()
        children(s + 1, p)
        exchange.finish()
        children(s + 1, 1 - p)
        low = factor(s + 1)
    copies.finish()


def local(targets, src_panels, live_counts, dest_owner, relative_map, diag_row, parent, chain_map):
    steps, _, rows, width = targets.shape
    src = src_panels.shape[0]
    cols = lax.axis_size("col")
    dest = dest_owner.T
    index = jnp.arange(src)
    ahead = (index // 16 - lax.axis_index("row")) % 4
    rank = jnp.where(ahead < 2, ahead, 5 - ahead) * 16 + index % 16
    alive = index < live_counts[0]
    before = (dest[:, :, None] == dest[:, None, :]) & (rank[None, :] < rank[:, None]) & alive
    pred = jnp.max(jnp.where(before, rank, -1), axis=2)
    pred = jnp.where(pred < 0, src, pred).astype(jnp.int32)
    mine = (dest[:, None, :] == jnp.arange(cols)[:, None]) & alive
    last = jnp.max(jnp.where(mine, rank, -1), axis=2)
    last = jnp.where(last < 0, src, last).astype(jnp.int32)
    copies = 6 + steps * 29 + (steps - 1) * 43
    out = pl.pallas_call(
        window_kernel,
        out_shape=jax.ShapeDtypeStruct((steps, rows, width), F32),
        in_specs=[ANY] * 9,
        out_specs=VMEM,
        scratch_shapes=[
            pltpu.SMEM(dest.shape, jnp.int32),
            pltpu.SMEM((steps, 2, src), jnp.int32),
            pltpu.SMEM(pred.shape, jnp.int32),
            pltpu.SMEM(last.shape, jnp.int32),
            pltpu.SMEM(diag_row.shape, jnp.int32),
            pltpu.SMEM(parent.shape, jnp.int32),
            pltpu.SMEM((steps - 1, 2, cols), jnp.int32),
            pltpu.VMEM((steps, rows, width), F32),
            pltpu.VMEM((src, 2, B, width), BF16),
            pltpu.VMEM((4, 8, B, width), BF16),
            pltpu.VMEM((4, 8, B, width), BF16),
            pltpu.VMEM((steps, 16, B, width), BF16),
            pltpu.VMEM((steps, 4, 16, B, width), BF16),
            pltpu.VMEM((src + 1, rows, width), F32),
            pltpu.VMEM((4, 4, rows, width), F32),
            pltpu.VMEM((4, 4, rows, width), F32),
            pltpu.VMEM((steps, 4, 4, rows, width), F32),
            pltpu.VMEM((steps, 2, 4, B, width), F32),
            pltpu.VMEM((steps, 2, 2, 2, B, width), F32),
            pltpu.VMEM((steps, 2, 2, 4, B, width), F32),
            pltpu.VMEM((steps, 2, 3, B, width), F32),
            pltpu.VMEM((steps, rows + B, width), F32),
            pltpu.SemaphoreType.DMA((11,)),
            pltpu.SemaphoreType.DMA((copies,)),
            pltpu.SemaphoreType.DMA((copies,)),
        ]
        + [pltpu.VMEM((4, B, width), F32)] * steps
        + [pltpu.VMEM((2, 4, 4, 2, 3, H, width), BF16)] * (steps - 1)
        + [pltpu.VMEM((4, 2, H, width), BF16)] * (steps - 1),
        compiler_params=pltpu.CompilerParams(collective_id=0, has_side_effects=True, vmem_limit_bytes=67_043_328),
        name="window",
    )(
        dest, relative_map.transpose(1, 2, 0), pred, last, diag_row, parent, chain_map.transpose(0, 2, 1),
        src_panels.reshape(src, 2, B, width), targets[:, 0],
    )
    return out[:, None]


def solution(mesh):
    return jax.shard_map(
        local,
        mesh=mesh,
        in_specs=(
            P(None, "col", "row", None),
            P("col", "row", None),
            P("col"),
            P("col", None),
            P("col", None, "row"),
            P(),
            P(),
            P(None, None, "row"),
        ),
        out_specs=P(None, "col", "row", None),
        check_vma=False,
    )
```

```python
import functools

import jax
import jax.numpy as jnp
from jax import lax
from jax.experimental import pallas as pl
from jax.experimental.pallas import tpu as pltpu
from jax.sharding import PartitionSpec as P

F32 = jnp.float32
BF16 = jnp.bfloat16
B = 128
H = B // 2
QUARTERS = (0, 1, 3, 2)
TRANS_B = (((1,), (1,)), ((), ()))
TRANS_A = (((0,), (0,)), ((), ()))
MESH = pl.DeviceIdType.MESH
VMEM = pl.BlockSpec(memory_space=pltpu.VMEM)
SMEM = pl.BlockSpec(memory_space=pltpu.SMEM)
ANY = pl.BlockSpec(memory_space=pl.ANY)


def split_product(left, right):
    def parts(v):
        high = v.astype(BF16).astype(F32)
        mid = (v - high).astype(BF16).astype(F32)
        return high, mid, v - high - mid

    lh, lm, ll = parts(left)
    rh, rm, rl = parts(right)
    lefts = jnp.concatenate([lh, lh, lm, lh, ll, lm], axis=0).astype(BF16)
    rights = jnp.concatenate([rh, rm, rh, rl, rh, rm], axis=0).astype(BF16)
    return lax.dot_general(lefts, rights, TRANS_A, preferred_element_type=F32)


def cholesky_inverse(a):
    n, nb = a.shape[0], 16
    lane = lax.broadcasted_iota(jnp.int32, (nb, n), 1)
    sub = lax.broadcasted_iota(jnp.int32, (nb, n), 0)
    upper, inverse = [], []
    next_a, next_w = a, None
    for j in range(n // nb):
        pa, rest_a = next_a[:nb], next_a[nb:]
        pw = (lane == sub + nb * j).astype(F32)
        if next_w is not None:
            pw = pw + next_w[:nb]
        cols = [jnp.broadcast_to(pa[:, nb * j + t : nb * j + t + 1], (nb, n)) for t in range(nb)]
        pivots = jnp.zeros((nb, n), F32)
        for t in range(nb):
            d = jnp.broadcast_to(cols[t][t : t + 1], (8, n))
            pivots = jnp.where(sub == t, jnp.concatenate([d, d], axis=0), pivots)
            if t < nb - 1:
                r = 1.0 / d
                ratio = jnp.where(sub > t, cols[t] * jnp.concatenate([r, r], axis=0), 0.0)
                for v in range(t + 1, nb):
                    cols[v] = cols[v] - ratio * cols[v][t : t + 1]
                pa = pa - ratio * pa[t : t + 1]
                pw = pw - ratio * pw[t : t + 1]
        scale = lax.rsqrt(pivots)
        scale = scale * (1.5 - 0.5 * pivots * scale * scale)
        pa = jnp.where(lane >= sub + nb * j, pa * scale, 0.0)
        pw = pw * scale
        upper.append(pa)
        inverse.append(pw)
        if j + 1 < n // nb:
            step = split_product(pa[:, nb * j + nb :], jnp.concatenate([pa, pw], axis=1))
            next_a = rest_a - step[:, :n]
            next_w = -step[:, n:] if next_w is None else next_w[nb:] - step[:, n:]
    return jnp.concatenate(upper, axis=0).T, jnp.concatenate(inverse, axis=0)


def position():
    me = lax.axis_index("col")
    return me // 8, lax.rem(me // 2, 4), lax.rem(me, 2), lax.axis_index("row")


def at_x(d):
    x, y, p, _ = position()
    return lax.rem(x + d, 4), {"col": (lax.rem(x + d, 4) * 4 + y) * 2 + p}


def at_y(d):
    x, y, p, _ = position()
    return lax.rem(y + d, 4), {"col": (x * 4 + lax.rem(y + d, 4)) * 2 + p}


def at_z(d):
    return {"row": lax.rem(lax.axis_index("row") + d, 4)}


def partner():
    x, y, p, _ = position()
    return {"col": (x * 4 + y) * 2 + 1 - p}


def greet(peers):
    barrier = pltpu.get_barrier_semaphore()
    for peer in peers:
        pl.semaphore_signal(barrier, inc=1, device_id=peer, device_id_type=MESH)
    pl.semaphore_wait(barrier, len(peers))


class Copies:
    def __init__(self, send, recv):
        self.send, self.recv, self.count, self.open = send, recv, 0, []

    def start(self, src, dst, peer):
        n = self.count
        copy = pltpu.make_async_remote_copy(
            src_ref=src, dst_ref=dst, send_sem=self.send.at[n], recv_sem=self.recv.at[n], device_id=peer, device_id_type=MESH
        )
        copy.start()
        self.count += 1
        self.open.append(copy)
        return copy

    def sent(self, copies):
        for copy in copies:
            copy.wait_send()
        self.open = [copy for copy in self.open if all(copy is not other for other in copies)]

    def finish(self):
        self.sent(self.open)


class Broadcast:
    def __init__(self, copies, mine, out):
        self.copies, self.mine, self.out = copies, mine, out
        self.up, self.down, self.on = [], [], []

    def start(self, part):
        row = lax.axis_index("row")
        blocks = pl.ds(part * 8, 8)
        self.up.append(self.copies.start(self.mine.at[blocks], self.out.at[row, blocks], at_z(1)))
        self.down.append(self.copies.start(self.mine.at[blocks], self.out.at[row, blocks], at_z(3)))

    def relay(self, part):
        row = lax.axis_index("row")
        self.up[part].wait_recv()
        ref = self.out.at[lax.rem(row + 3, 4), pl.ds(part * 8, 4)]
        self.on.append(self.copies.start(ref, ref, at_z(1)))
        self.down[part].wait_recv()
        ref = self.out.at[lax.rem(row + 1, 4), pl.ds(part * 8 + 4, 4)]
        self.on.append(self.copies.start(ref, ref, at_z(3)))

    def finish(self):
        for copy in self.on:
            copy.wait_recv()


class Exchange:
    rows, head = slice(0, 2), slice(2, 3)

    def __init__(self, copies, low, out, zbuf):
        self.copies, self.out, self.zbuf = copies, out, zbuf
        x, y, p, row = position()
        for h in range(2):
            zbuf[row, h] = low[B + h * H : B + (h + 1) * H]
        for h in range(2):
            for b in range(2):
                out[h, x, y, p, b] = low[b * B + h * H : b * B + (h + 1) * H]

    def line(self, h, fixed, what):
        p = position()[2]
        return self.out.at[1, fixed, :, p, what] if h else self.out.at[0, :, fixed, p, what]

    def open_half(self, h, what, src):
        x, y, p, _ = position()
        move = at_y if h else at_x
        return [self.copies.start(src, self.out.at[h, x, y, p, what], move(d)[1]) for d in (2, 1, 3)]

    def begin(self):
        x, y, p, row = position()
        self.heads = [self.copies.start(self.zbuf.at[row], self.zbuf.at[row], at_z(d)) for d in (2, 1, 3)]
        self.opened = [self.open_half(h, self.rows, self.out.at[h, x, y, p, self.rows]) for h in range(2)]

    def pick(self, root):
        x, y, p, _ = position()
        for copy in self.heads:
            copy.wait_recv()
        picked = self.zbuf[root]
        for h in range(2):
            self.out[h, x, y, p, 2] = picked[h]
        self.opened_head = [self.open_half(h, self.head, self.out.at[h, x, y, p, self.head]) for h in range(2)]

    def turn_half(self, h, what, opened):
        x, y, _, _ = position()
        for copy in opened:
            copy.wait_recv()
        move, here = (at_x, x) if h else (at_y, y)
        ref = self.line(h, here, what)
        return [self.copies.start(ref, ref, move(d)[1]) for d in (2, 1, 3)], self.copies.start(ref, ref, partner())

    def turn_rows(self):
        self.turned = [self.turn_half(h, self.rows, self.opened[h]) for h in range(2)]

    def turn_head(self):
        self.turned_head = [self.turn_half(h, self.head, self.opened_head[h]) for h in range(2)]

    def close_half(self, h, what, turned):
        self.done.append(turned[1])
        move = at_x if h else at_y
        for d, copy in zip((2, 1, 3), turned[0]):
            copy.wait_recv()
            ref = self.line(h, move(4 - d)[0], what)
            self.done.append(self.copies.start(ref, ref, partner()))

    def close_rows(self):
        self.done = []
        for h in range(2):
            self.close_half(h, self.rows, self.turned[h])

    def close_head(self):
        for h in range(2):
            self.close_half(h, self.head, self.turned_head[h])

    def finish(self):
        for copy in self.done:
            copy.wait_recv()


class Reduce:
    def __init__(self, copies, acc, away, in0, part, far, in1, in2, zbuf):
        self.copies, self.acc, self.away, self.far = copies, acc, away, far
        self.in0, self.part, self.in1, self.in2, self.zbuf = in0, part, in1, in2, zbuf

    def begin(self, previous, sums, slot):
        p = position()[2]
        if previous is not None:
            self.copies.sent(previous.first)
        self.own = lambda i: sums[slot(i * 2 + p)]
        self.first = []
        for d in (2, 1, 3, 0):
            to = at_x(d)[0]

            @pl.loop(0, 4)
            def _(i):
                self.away[to, i] = sums[slot((to * 4 + i) * 2 + 1 - p)]

            self.first.append(self.copies.start(self.away.at[to], self.in0.at[to], partner()))

    def pair(self, previous):
        if previous is not None:
            self.copies.sent(previous.opened + previous.second)
        acc, in0, far = self.acc, self.in0, self.far
        self.opened = []
        for d, first in zip((2, 1, 3, 0), self.first):
            to = at_x(d)[0]
            first.wait_recv()

            @pl.loop(0, 4)
            def _(i):
                acc[to, i] = self.own(to * 4 + i) + in0[to, i]

            if d == 2:
                self.opened.append(self.copies.start(acc.at[to, :2, :B], far.at[0, 0], at_x(1)[1]))
                self.opened.append(self.copies.start(acc.at[to, 2:, :B], far.at[0, 1], at_x(3)[1]))
        to = at_y(2)[0]
        self.opened.append(self.copies.start(acc.at[:2, to, B:], far.at[1, 0], at_y(1)[1]))
        self.opened.append(self.copies.start(acc.at[2:, to, B:], far.at[1, 1], at_y(3)[1]))

    def combine(self):
        for copy in self.opened:
            copy.wait_recv()
        acc, far, in1 = self.acc, self.far, self.in1
        self.second = []
        for n, d in enumerate((1, 3)):
            (to_x, peer_x), (to_y, peer_y) = at_x(d), at_y(d)
            for i in range(2):
                acc[to_x, 2 * n + i, :B] += far[0, n, i]
                acc[2 * n + i, to_y, B:] += far[1, n, i]
            self.second.append(self.copies.start(acc.at[to_x, :, :B], in1.at[0, n], peer_x))
            self.second.append(self.copies.start(acc.at[:, to_y, B:], in1.at[1, n], peer_y))

    def cross(self):
        x, y, _, _ = position()
        for copy in self.second:
            copy.wait_recv()
        acc, in1, part = self.acc, self.in1, self.part

        @pl.loop(0, 4)
        def _(i):
            part[0, i] = acc[x, i, :B] + (in1[0, 0, i] + in1[0, 1, i])
            part[1, i] = acc[i, y, B:] + (in1[1, 0, i] + in1[1, 1, i])

        self.third = []
        for d in (2, 1, 3):
            to, peer = at_y(d)
            self.third.append(self.copies.start(part.at[0, to], self.in2.at[0, d - 1], peer))
            to, peer = at_x(d)
            self.third.append(self.copies.start(part.at[1, to], self.in2.at[1, d - 1], peer))

    def finish(self, target, base):
        x, y, _, row = position()
        for copy in self.third:
            copy.wait_recv()
        part, in2, zbuf = self.part, self.in2, self.zbuf
        top = target[:B] - (part[0, y] + in2[0, 0] + in2[0, 1] + in2[0, 2])
        zbuf[row] = top
        base[:B] = top
        base[B:] = target[B:] - (part[1, x] + in2[1, 0] + in2[1, 1] + in2[1, 2])
        self.fourth = [self.copies.start(zbuf.at[row], zbuf.at[row], at_z(d)) for d in (2, 1, 3)]

    def diagonal(self, root):
        for copy in self.fourth:
            copy.wait_recv()
        return self.zbuf[root]


def window_kernel(
    dest_hbm, map_hbm, pred_hbm, last_hbm, root_hbm, parent_hbm, chain_hbm, panel_hbm, target_hbm, out_ref,
    dest_ref, map_ref, pred_ref, last_ref, root_ref, parent_ref, chain_ref, target_ref,
    panels, zb0, zb1, chosen, heads, sums, away, acc, in0, part, far, in1, in2, upd, load_sem, send_sem, recv_sem, *bufs,
):
    steps = target_ref.shape[0]
    diags, child, headbuf = bufs[:steps], bufs[steps : 2 * steps - 1], bufs[2 * steps - 1 :]
    src = panels.shape[0]
    x, y, p, row = position()
    me = lax.axis_index("col")
    copies = Copies(send_sem, recv_sem)
    load = pltpu.make_async_copy(panel_hbm, panels, load_sem.at[0])

    def quarter(q, part):
        return panel_hbm.at[pl.ds(q * 16 + part * 8, 8), 0]

    tables = [
        pltpu.make_async_copy(a, b, load_sem.at[3 + n])
        for n, (a, b) in enumerate(
            (
                (dest_hbm, dest_ref), (map_hbm, map_ref), (pred_hbm, pred_ref), (last_hbm, last_ref),
                (root_hbm, root_ref), (parent_hbm, parent_ref), (chain_hbm, chain_ref), (target_hbm, target_ref),
            )
        )
    ]
    zb = (zb0, zb1)
    own = [pltpu.make_async_copy(quarter(row, i), zb[i].at[row], load_sem.at[1 + i]) for i in range(2)]
    for copy in own:
        copy.start()
    sums[src] = jnp.zeros(sums.shape[1:], F32)
    greet([partner()] + [at_z(d) for d in (1, 2, 3)] + [f(d)[1] for f in (at_x, at_y) for d in (1, 2, 3)])
    opened = [[copies.start(quarter(lax.rem(row + d, 4), i), zb[i].at[row], at_z(d)) for d in (2, 1, 3)] for i in range(2)]
    for table in tables:
        table.start()
    load.start()
    for table in tables:
        table.wait()

    def choose(s, part):
        @pl.loop(0, 8)
        def _(j):
            i = part * 8 + j
            chosen[s, i] = zb[part][root_ref[s, dest_ref[s, row * 16 + i]], j]

    def keep(s):
        @pl.loop(0, 16)
        def _(j):
            heads[s, row, j] = chosen[s, j]

    def products(s, place):
        quarter = lax.rem(row + QUARTERS[place], 4)

        @pl.loop(0, 4)
        def _(g):
            prods = []
            for u in range(4):
                i = quarter * 16 + g * 4 + u
                first = map_ref[s, 0, i]
                block = jnp.concatenate([panels[i, first], panels[i, 1 - first]], axis=0)
                prods.append(
                    lax.dot_general(block, heads[s, quarter, g * 4 + u], TRANS_B, preferred_element_type=F32)
                )
            for u in range(4):
                i = quarter * 16 + g * 4 + u
                sums[place * 16 + g * 4 + u] = prods[u] + sums[pred_ref[s, i]]

    reduces = [
        Reduce(copies, acc, away, in0.at[s], part.at[s], far.at[s], in1.at[s], in2.at[s], diags[s]) for s in range(steps)
    ]
    casts = [Broadcast(copies, chosen.at[s], heads.at[s]) for s in range(steps)]

    def begin(s):
        reduces[s].begin(reduces[s - 1] if s else None, sums, lambda c: last_ref[s, c])

    def children(s, parity):
        @pl.loop(0, 8)
        def _(g):
            lefts, rights = [], []
            for u in range(2):
                a, b = g // 2, lax.rem(g, 2) * 2 + u
                k = (a * 4 + b) * 2 + parity
                mine = parent_ref[s - 1, k] == me
                head = jnp.concatenate([child[s - 1][h, a, b, parity, 2] for h in range(2)], axis=0)
                head = jnp.where(mine, head, jnp.zeros_like(head))
                first = chain_ref[s - 1, 0, k]
                left_out = root_ref[s - 1, k] == row
                blocks = [jnp.concatenate([child[s - 1][h, a, b, parity, q] for h in range(2)], axis=0) for q in range(2)]
                blocks[0] = jnp.where(left_out, jnp.zeros_like(blocks[0]), blocks[0])
                blocks = [jnp.where(first == q, blocks[0], blocks[1]) for q in range(2)]
                lefts.append(jnp.concatenate(blocks + [head], axis=0))
                rights.append(head)
            upd[s] -= lax.dot_general(
                jnp.concatenate(lefts, axis=1), jnp.concatenate(rights, axis=1), TRANS_B, preferred_element_type=F32
            )

    def factor(s):
        lower, inverse = cholesky_inverse(upd[s, 2 * B :])
        solved = lax.dot_general(
            upd[s, : 2 * B], inverse, TRANS_B, precision=lax.Precision.HIGHEST, preferred_element_type=F32
        )
        top = jnp.where(root_ref[s, me] == row, lower, solved[:B])
        panel = jnp.concatenate([top, solved[B:]], axis=0)
        out_ref[s] = panel
        return panel.astype(BF16)

    def both(action):
        for part in range(2):
            action(part)

    for part in range(2):
        own[part].wait()
        for copy in opened[part]:
            copy.wait_recv()
        choose(0, part)
        casts[0].start(part)
    keep(0)
    for s in range(1, steps):
        for part in range(2):
            choose(s, part)
        keep(s)
    load.wait()
    products(0, 0)
    both(casts[0].relay)
    both(casts[1].start)
    products(0, 1)
    products(0, 2)
    casts[0].finish()
    products(0, 3)
    begin(0)
    reduces[0].pair(None)
    casts[1].relay(0)
    reduces[0].combine()
    casts[1].relay(1)
    casts[2].start(0)
    for place in range(3):
        products(1, place)
    casts[1].finish()
    products(1, 3)
    begin(1)
    reduces[0].cross()
    reduces[1].pair(reduces[0])
    casts[2].relay(0)
    reduces[0].finish(target_ref.at[0], upd.at[0, : 2 * B])
    casts[2].start(1)
    reduces[1].combine()
    upd[0, 2 * B :] = reduces[0].diagonal(root_ref[0, me])
    low = factor(0)
    for s in range(steps - 1):
        ahead = s + 2 if s + 2 < steps else None
        exchange = Exchange(copies, low, child[s], headbuf[s])
        exchange.begin()
        exchange.pick(root_ref[s + 1, parent_ref[s, me]])
        if ahead:
            casts[ahead].relay(1)
        if s + 3 < steps:
            casts[s + 3].start(0)
        reduces[s + 1].cross()
        exchange.turn_rows()
        if ahead:
            products(ahead, 0)
            products(ahead, 1)
        exchange.turn_head()
        if ahead:
            products(ahead, 2)
            casts[ahead].finish()
            products(ahead, 3)
            begin(ahead)
        reduces[s + 1].finish(target_ref.at[s + 1], upd.at[s + 1, : 2 * B])
        if s + 3 < steps:
            casts[s + 3].relay(0)
            casts[s + 3].start(1)
        if ahead:
            reduces[ahead].pair(reduces[ahead - 1])
        exchange.close_rows()
        exchange.close_head()
        upd[s + 1, 2 * B :] = reduces[s + 1].diagonal(root_ref[s + 1, me])
        if ahead:
            reduces[ahead].combine()
        children(s + 1, p)
        exchange.finish()
        children(s + 1, 1 - p)
        low = factor(s + 1)
    copies.finish()


def local(targets, src_panels, live_counts, dest_owner, relative_map, diag_row, parent, chain_map):
    steps, _, rows, width = targets.shape
    src = src_panels.shape[0]
    cols = lax.axis_size("col")
    dest = dest_owner.T
    index = jnp.arange(src)
    ahead = (index // 16 - lax.axis_index("row")) % 4
    rank = jnp.where(ahead < 2, ahead, 5 - ahead) * 16 + index % 16
    alive = index < live_counts[0]
    before = (dest[:, :, None] == dest[:, None, :]) & (rank[None, :] < rank[:, None]) & alive
    pred = jnp.max(jnp.where(before, rank, -1), axis=2)
    pred = jnp.where(pred < 0, src, pred).astype(jnp.int32)
    mine = (dest[:, None, :] == jnp.arange(cols)[:, None]) & alive
    last = jnp.max(jnp.where(mine, rank, -1), axis=2)
    last = jnp.where(last < 0, src, last).astype(jnp.int32)
    copies = 6 + steps * 29 + (steps - 1) * 43
    out = pl.pallas_call(
        window_kernel,
        out_shape=jax.ShapeDtypeStruct((steps, rows, width), F32),
        in_specs=[ANY] * 9,
        out_specs=VMEM,
        scratch_shapes=[
            pltpu.SMEM(dest.shape, jnp.int32),
            pltpu.SMEM((steps, 2, src), jnp.int32),
            pltpu.SMEM(pred.shape, jnp.int32),
            pltpu.SMEM(last.shape, jnp.int32),
            pltpu.SMEM(diag_row.shape, jnp.int32),
            pltpu.SMEM(parent.shape, jnp.int32),
            pltpu.SMEM((steps - 1, 2, cols), jnp.int32),
            pltpu.VMEM((steps, rows, width), F32),
            pltpu.VMEM((src, 2, B, width), BF16),
            pltpu.VMEM((4, 8, B, width), BF16),
            pltpu.VMEM((4, 8, B, width), BF16),
            pltpu.VMEM((steps, 16, B, width), BF16),
            pltpu.VMEM((steps, 4, 16, B, width), BF16),
            pltpu.VMEM((src + 1, rows, width), F32),
            pltpu.VMEM((4, 4, rows, width), F32),
            pltpu.VMEM((4, 4, rows, width), F32),
            pltpu.VMEM((steps, 4, 4, rows, width), F32),
            pltpu.VMEM((steps, 2, 4, B, width), F32),
            pltpu.VMEM((steps, 2, 2, 2, B, width), F32),
            pltpu.VMEM((steps, 2, 2, 4, B, width), F32),
            pltpu.VMEM((steps, 2, 3, B, width), F32),
            pltpu.VMEM((steps, rows + B, width), F32),
            pltpu.SemaphoreType.DMA((11,)),
            pltpu.SemaphoreType.DMA((copies,)),
            pltpu.SemaphoreType.DMA((copies,)),
        ]
        + [pltpu.VMEM((4, B, width), F32)] * steps
        + [pltpu.VMEM((2, 4, 4, 2, 3, H, width), BF16)] * (steps - 1)
        + [pltpu.VMEM((4, 2, H, width), BF16)] * (steps - 1),
        compiler_params=pltpu.CompilerParams(collective_id=0, has_side_effects=True, vmem_limit_bytes=67_043_328),
        name="window",
    )(
        dest, relative_map.transpose(1, 2, 0), pred, last, diag_row, parent, chain_map.transpose(0, 2, 1),
        src_panels.reshape(src, 2, B, width), targets[:, 0],
    )
    return out[:, None]


def solution(mesh):
    return jax.shard_map(
        local,
        mesh=mesh,
        in_specs=(
            P(None, "col", "row", None),
            P("col", "row", None),
            P("col"),
            P("col", None),
            P("col", None, "row"),
            P(),
            P(),
            P(None, None, "row"),
        ),
        out_specs=P(None, "col", "row", None),
        check_vma=False,
    )
```
